512 devices in a mesh: dom: 128 (over y, z, core), rep: 4 (over x).
Axes of the slice: x: 4, y: 8, z: 8, core: 2. Of those that a mesh axis runs over, the one named last changes fastest.
Arguments:
- entities: bfloat16 [32768, 400], P('dom'), may hold values from -2.5 to 2.5, as said below
- relation: float32 [1000, 400], replicated, may hold values from 0.25 to 1.75
- serve_ids: int32 [128, 128, 2], P('dom'), may hold values from 0 to 255
- edge_src: int32 [128, 4, 512], P('dom', 'rep'), may hold values from 0 to 255
- edge_rel: int32 [128, 4, 512], P('dom', 'rep'), may hold values from 0 to 999
- edge_dst: int32 [128, 4, 512], P('dom', 'rep'), may hold values from 0 to 255
- neg_ids: int32 [128, 4, 2, 384], P('dom', 'rep'), may hold values from 0 to 255
- edge_count: int32 [128, 4], P('dom', 'rep'), may hold values from 1 to 512, 1536 in all within a row
Outputs:
- entity_grad: float32 [32768, 400], P('dom', 'rep')
- relation_grad: float32 [1000, 400], replicated
The draws below stay inside these ranges and needn't reach their ends.
Inputs may be any that keep to these rules, and one draw needn't show every extreme that they name: `entities`: entity entries are bounded.
All inputs are finite; a program needn't handle non-finite values. No bound on the sum of `edge_count` on one device may be relied on, other than what follows from the above.
Results may differ from the reference program's by a relative error of at most 0.0021.
The reference program's roundings to bfloat16 on the way count: a program that leaves them out, or rounds other values in their place, can miss the bound.
Values may be sent and summed in bfloat16 or wider, within the bound.
A program may use at most 64 MiB of HBM per device.

```python
import math
import jax
import jax.numpy as jnp
import numpy as np
from jax import lax

D = 400
NREL = 1000
ENT_DEV = 256
CAP = 2
EDGE_DEV = 512
NEG = 384
WORKERS = 128
REPS = 4
ENTITIES = 32768
GROUPS = 2


def draw_entities(key, part):
    first = jax.random.fold_in(key, 0)
    values = 0.3 * jax.random.truncated_normal(first, -4.0, 4.0, (ENTITIES, D), jnp.float32)
    return values.astype(jnp.bfloat16)


def set_ends(entries, rng, low, top_value):
    spot = [jax.random.randint(jax.random.fold_in(rng, axis), (), 0, length) for axis, length in enumerate(entries.shape)]
    longest = entries.shape.index(max(entries.shape))
    neighbour = spot[:longest] + [(spot[longest] + 1) % entries.shape[longest]] + spot[longest + 1:]
    return entries.at[tuple(spot)].set(low).at[tuple(neighbour)].set(top_value)


def rank_bounds(count, slope):
    weights = [(1 << 20) // math.isqrt(grade ** slope) + 1 for grade in range(1, count + 1)]
    scale = 1 + sum(weights) // (1 << 30)
    return np.cumsum(np.array([max(1, weight // scale) for weight in weights]))


def ranked(stream_key, extent, number_of, slope):
    grid = rank_bounds(number_of, slope)
    lot = jax.random.randint(jax.random.fold_in(stream_key, 1), extent, 0, int(grid[number_of - 1]))
    rank = jnp.searchsorted(jnp.asarray(grid, jnp.int32), lot, side="right")
    return jax.random.permutation(jax.random.fold_in(stream_key, 2), number_of)[rank].astype(jnp.int32)


def length_profile(number_of, total, limit, slope):
    portions = [(1 << 20) // math.isqrt(standing ** slope) + 1 for standing in range(2, number_of + 1)]
    rest, counts = total - limit - (number_of - 1), [1] * (number_of - 1)
    while rest > 0:
        free = [i for i in range(number_of - 1) if counts[i] < limit]
        pool, left = sum([portions[i] for i in free]), rest
        for i in free:
            addition = min(limit - counts[i], max(1, left * portions[i] // pool), rest)
            counts[i] = counts[i] + addition
            rest = rest - addition
    return np.array([limit] + counts)


def uneven(rng, count, total, bound, skew):
    if count == 2:
        one = jax.random.randint(rng, (), max(1, total - bound), min(bound, total - 1) + 1)
        return jnp.stack([one, total - one])
    tallies = jnp.asarray(length_profile(count, total, bound, skew), jnp.int32)
    pairs = (count - 1) // 2
    donor, taker = tallies[1:1 + 2 * pairs:2], tallies[2:2 + 2 * pairs:2]
    room = jnp.minimum(donor - 1, bound - taker)
    shifted = jax.random.randint(jax.random.fold_in(rng, 1), (pairs,), 0, 1 << 20) % (room + 1)
    tallies = tallies.at[1:1 + 2 * pairs:2].set(donor - shifted).at[2:2 + 2 * pairs:2].set(taker + shifted)
    return tallies[jax.random.permutation(jax.random.fold_in(rng, 2), count)]


def setup_inputs(seed: int = 0) -> dict:
    streams_of = jax.random.split(jax.random.key(seed), 9)
    return {
        "entities": draw_entities(jax.random.fold_in(streams_of[8], 71), 0),
        "relation": jnp.clip(jax.random.uniform(streams_of[1], (NREL, D), jnp.float32, 0.25, 1.75), 0.25, 1.75),
        "serve_ids": set_ends(jax.random.randint(streams_of[2], (WORKERS, WORKERS, CAP), 0, ENT_DEV), jax.random.fold_in(streams_of[2], 1), 0, ENT_DEV - 1).astype(jnp.int32),
        "edge_src": set_ends(jax.random.randint(streams_of[3], (WORKERS, REPS, EDGE_DEV), 0, ENT_DEV), jax.random.fold_in(streams_of[3], 1), 0, ENT_DEV - 1).astype(jnp.int32),
        "edge_rel": set_ends(ranked(streams_of[4], (WORKERS, REPS, EDGE_DEV), NREL, 2), jax.random.fold_in(streams_of[4], 3), 0, NREL - 1).astype(jnp.int32),
        "edge_dst": set_ends(jax.random.randint(streams_of[5], (WORKERS, REPS, EDGE_DEV), 0, WORKERS * CAP), jax.random.fold_in(streams_of[5], 1), 0, (WORKERS * CAP) - 1).astype(jnp.int32),
        "neg_ids": set_ends(jax.random.randint(streams_of[6], (WORKERS, REPS, GROUPS, NEG), 0, WORKERS * CAP), jax.random.fold_in(streams_of[6], 1), 0, (WORKERS * CAP) - 1).astype(jnp.int32),
        "edge_count": jax.vmap(lambda own: uneven(own, REPS, 3 * EDGE_DEV, EDGE_DEV, 2))(jax.random.split(streams_of[7], WORKERS)).reshape((WORKERS, REPS)).astype(jnp.int32),
    }


def shard_grads(lhs_block, relation, table, src, rel, dst, neg, count):
    groups = neg.shape[0]
    edges = src.shape[0]
    width = edges // groups
    lhs_rows = lhs_block[src].astype(jnp.float32)
    rel_rows = relation[rel]
    query = (lhs_rows * rel_rows).astype(jnp.bfloat16).reshape(groups, width, -1)
    cands = jnp.concatenate([table[dst].reshape(groups, width, -1), table[neg]], axis=1)
    scores = jnp.einsum("cid,cjd->cij", query.astype(jnp.float32), cands.astype(jnp.float32))
    position = jnp.arange(edges, dtype=jnp.int32).reshape(groups, width)
    live = position < count
    columns = jnp.concatenate([live, jnp.ones((groups, neg.shape[1]), dtype=bool)], axis=1)
    scores = jnp.where(columns[:, None, :], scores, jnp.float32(-1e30))
    top = jnp.max(scores, axis=-1, keepdims=True)
    expo = jnp.exp(scores - top)
    probs = expo / jnp.sum(expo, axis=-1, keepdims=True)
    onehot = (jnp.arange(width + neg.shape[1])[None, :] == jnp.arange(width)[:, None]).astype(jnp.float32)
    grads = ((probs - onehot[None]) * live[:, :, None].astype(jnp.float32)).astype(jnp.bfloat16)
    dquery = jnp.einsum("cij,cjd->cid", grads.astype(jnp.float32), cands.astype(jnp.float32)).reshape(edges, -1)
    dcand = jnp.einsum("cij,cid->cjd", grads.astype(jnp.float32), query.astype(jnp.float32))
    dim = lhs_block.shape[1]
    lhs_grad = jnp.zeros(lhs_block.shape, jnp.float32).at[src].add(dquery * rel_rows)
    rel_grad = jnp.zeros(relation.shape, jnp.float32).at[rel].add(dquery * lhs_rows)
    table_grad = jnp.zeros(table.shape, jnp.float32).at[dst].add(dcand[:, :width].reshape(edges, dim))
    table_grad = table_grad.at[neg.reshape(-1)].add(dcand[:, width:].reshape(-1, dim))
    return lhs_grad, table_grad, rel_grad


def reference(entities, relation, serve_ids, edge_src, edge_rel, edge_dst, neg_ids, edge_count):
    workers = serve_ids.shape[0]
    cap = serve_ids.shape[2]
    dim = entities.shape[1]
    blocks = entities.reshape(workers, -1, dim)
    owners = jnp.arange(workers, dtype=jnp.int32)

    def one_worker(items):
        worker, src, rel, dst, neg, count = items
        picked = serve_ids[:, worker, :]
        table = blocks[owners[:, None], picked].reshape(workers * cap, dim)
        lhs_block = blocks[worker]
        lhs_grad, table_grad, rel_grad = jax.vmap(shard_grads, in_axes=(None, None, None, 0, 0, 0, 0, 0))(lhs_block, relation, table, src, rel, dst, neg, count)
        return jnp.sum(lhs_grad, axis=0), jnp.sum(table_grad, axis=0), jnp.sum(rel_grad, axis=0)

    lhs_all, table_all, rel_all = lax.map(one_worker, (owners, edge_src, edge_rel, edge_dst, neg_ids, edge_count))
    table_all = jnp.transpose(table_all.reshape(workers, workers, cap, dim), (1, 0, 2, 3))

    def own_rows(lhs_grad, served, grads):
        return lhs_grad.at[served.reshape(-1)].add(grads.reshape(-1, dim))

    entity_grad = jax.vmap(own_rows)(lhs_all, serve_ids, table_all).reshape(-1, dim)
    slots = edge_src.shape[0] * edge_src.shape[1] * edge_src.shape[2]
    relation_grad = jnp.sum(rel_all, axis=0) / jnp.float32(slots)
    return entity_grad, relation_grad
```

```python
import jax
import jax.numpy as jnp
from jax import lax
from jax.experimental import pallas as pl
from jax.experimental.pallas import tpu as pltpu
from jax.sharding import PartitionSpec as P

F32 = jnp.float32
BF16 = jnp.bfloat16
I32 = jnp.int32
NX, NY, NZC = 4, 8, 16
D, NREL, RELP = 400, 1000, 1024
SLOTS, EDGES, BLOCK, GROUPS = 256, 512, 256, 2
QUARTER = 100
PART_A, PART_B = 104, 96
PAIR = {
    "a1": 7, "a2": 15, "b1": 15, "b2": 7,
    "core": 2, "s1a": 7, "s1b": 7, "s2a": 7, "s2b": 7, "s3": 3,
    "s4a": 7, "s4b": 7, "s5a": 7, "s5b": 7, "s6": 16,
    "tx": 3, "lx": 3, "ry": 7, "rz": 15,
}
FIRST = {}
for _name, _number in PAIR.items():
    FIRST[_name] = sum(list(PAIR.values())[: len(FIRST)])
COPIES = sum(PAIR.values())


def nn(a, b):
    return jnp.dot(a, b, preferred_element_type=F32)


def nt(a, b):
    return lax.dot_general(a, b, (((1,), (1,)), ((), ())), preferred_element_type=F32)


def split2(v):
    hi = v.astype(BF16)
    return hi, (v - hi.astype(F32)).astype(BF16)


def onehot(shape, axis, ids):
    return jnp.where(lax.broadcasted_iota(I32, shape, axis) == ids, F32(1), F32(0))


def kernel(
    ent, rel_hbm, serve, src, rel, dst, neg, count,
    out_ent, gath,
    relv, outs, outp, ra1, ra1p, ra2, rb1, rb1p, tab, perm, permt, ohsp,
    ohsrc, ohrel, fbuf, lhsv, relr, query, query4,
    rg, crecv, rgs, a1, a1s, b1, b1s, a2, b2, s3, ga, gb,
    tg, tgr, tgs, ryb, rzs, rzb, lg, lgr,
    relsem, ssem, rsem,
):
    me, x = lax.axis_index("dom"), lax.axis_index("rep")
    y, zc = me // NZC, lax.rem(me, NZC)
    z, c = zc // 2, lax.rem(zc, 2)

    def to_y(d):
        return {"dom": lax.rem(y + d, NY) * NZC + zc, "rep": x}

    def to_zc(d):
        return {"dom": y * NZC + lax.rem(zc + d, NZC), "rep": x}

    def to_z(d):
        return {"dom": y * NZC + lax.rem(z + d, NY) * 2 + c, "rep": x}

    def to_x(d):
        return {"dom": me, "rep": lax.rem(x + d, NX)}

    to_core = {"dom": y * NZC + z * 2 + 1 - c, "rep": x}
    started = []

    def send(stage, i, source, target, device):
        n = FIRST[stage] + i
        copy = pltpu.make_async_remote_copy(
            src_ref=source, dst_ref=target, send_sem=ssem.at[n], recv_sem=rsem.at[n],
            device_id=device, device_id_type=pl.DeviceIdType.MESH,
        )
        copy.start()
        started.append(copy)
        return copy

    def landed(copies):
        for copy in copies:
            copy.wait_recv()

    barrier = pltpu.get_barrier_semaphore()
    partners = [to_y(d) for d in range(1, NY)] + [to_zc(d) for d in range(1, NZC)]
    partners += [to_x(d) for d in range(1, NX)]
    for device in partners:
        pl.semaphore_signal(barrier, inc=1, device_id=device, device_id_type=pl.DeviceIdType.MESH)

    fetch = pltpu.make_async_copy(rel_hbm, relv, relsem)
    fetch.start()

    row = lax.broadcasted_iota(I32, (SLOTS, SLOTS), 0)
    col = lax.broadcasted_iota(I32, (SLOTS, SLOTS), 1)
    moved = lax.rem(col, 16) * 16 + (col // 128) * 8 + lax.rem(col // 16, 8)
    perm[...] = jnp.where(row == moved, F32(1), F32(0)).astype(BF16)
    moved = lax.rem(row, 16) * 16 + (row // 128) * 8 + lax.rem(row // 16, 8)
    permt[...] = jnp.where(col == moved, F32(1), F32(0)).astype(BF16)
    served = jnp.concatenate([serve[0:1, :], serve[1:2, :]], axis=1)
    ohst = jnp.where(row == served, F32(1), F32(0))
    ohs = ohst.T.astype(BF16)
    outs[:, :, 384:512] = jnp.zeros((2, 128, 128), BF16)
    outs[:, :, 0:D] = nt(ohs, ent[...]).astype(BF16).reshape(2, 128, D)
    outp[:, 128:256] = jnp.zeros((SLOTS, 128), BF16)
    outp[:, 0 : D - 256] = nn(perm[...], outs[:, :, 256:D].reshape(SLOTS, D - 256)).astype(BF16)

    pl.semaphore_wait(barrier, len(partners))

    def y_rows(index):
        return pl.ds(pl.multiple_of(index * 16, 16), 16)

    ca1, cb1 = [], []
    for d in range(1, NY):
        to = lax.rem(y + d, NY)
        ca1.append(send("a1", d - 1, outs.at[:, y_rows(to), 0:256], ra1.at[:, y_rows(y), :], to_y(d)))
    for d in range(1, NZC):
        to = lax.rem(zc + d, NZC)
        cb1.append(send("b1", d - 1, outp.at[y_rows(to), :], rb1.at[y_rows(zc), :], to_zc(d)))
    ra1[:, y_rows(y), :] = outs[:, y_rows(y), 0:256]
    rb1[y_rows(zc), :] = outp[y_rows(zc), :]

    ohsp[...] = nt(ohst.astype(BF16), perm[...]).astype(BF16)
    ohsrc[...] = onehot((SLOTS, EDGES), 0, src[...]).astype(BF16)
    fbuf[...] = nn(ent[...], ohsrc[...])
    lhsv[...] = fbuf[...]
    ohrel[...] = onehot((RELP, EDGES), 0, rel[...]).astype(BF16)
    fetch.wait()
    for q in range(4):
        part = relv[q * 104 : min(D, q * 104 + 104), :]
        hi = part.astype(BF16)
        rest = part - hi.astype(F32)
        mid = rest.astype(BF16)
        low = (rest - mid.astype(F32)).astype(BF16)
        picks = ohrel[0:NREL, :]
        relr[q * 104 : min(D, q * 104 + 104), :] = (nn(hi, picks) + nn(mid, picks)) + nn(low, picks)
    fbuf[...] = lhsv[...] * relr[...]
    query[...] = fbuf[...].astype(BF16)
    query4[...] = jnp.zeros(query4.shape, BF16)
    for q in range(4):
        query4[q, 0:QUARTER, :] = fbuf[q * QUARTER : (q + 1) * QUARTER, :].astype(BF16)

    live = lax.broadcasted_iota(I32, (1, EDGES), 1) < count[0, 0]
    livef = jnp.where(live, F32(1), F32(0))
    dsts = lax.rem(dst[...], 2) * 128 + dst[...] // 2
    negs = lax.rem(neg[...], 2) * 128 + neg[...] // 2
    ohdst = onehot((SLOTS, EDGES), 0, dsts) * livef
    times = []
    for b in range(GROUPS):
        ohneg = onehot((SLOTS, negs.shape[1]), 0, negs[b : b + 1, :])
        own = ohdst[:, b * BLOCK : (b + 1) * BLOCK]
        times.append(
            jnp.sum(ohneg, axis=1, keepdims=True) + jnp.sum(own, axis=1, keepdims=True)
        )

    landed(ca1)
    ra1p[...] = nn(perm[...], ra1[...].reshape(SLOTS, 256)).astype(BF16)
    ca2 = []
    for d in range(1, NZC):
        to = lax.rem(zc + d, NZC)
        ca2.append(send("a2", d - 1, ra1p.at[y_rows(to), :], ra2.at[y_rows(zc), :], to_zc(d)))
    ra2[y_rows(zc), :] = ra1p[y_rows(zc), :]
    landed(cb1)
    rb1p[...] = nn(permt[...], rb1[...]).astype(BF16).reshape(2, 128, 256)
    cb2 = []
    for d in range(1, NY):
        to = lax.rem(y + d, NY)
        cb2.append(
            send("b2", d - 1, rb1p.at[:, y_rows(to), :], tab.at[:, y_rows(y), 256:512], to_y(d))
        )
    tab[:, y_rows(y), 256:512] = rb1p[:, y_rows(y), :]
    landed(ca2)
    tab[:, :, 0:256] = nn(permt[...], ra2[...]).astype(BF16).reshape(2, 128, 256)
    landed(cb2)

    table = tab[...].reshape(SLOTS, 512)
    scores = nn(table[:, 0:D], query[...])
    his, los = [], []
    for b in range(GROUPS):
        span = slice(b * BLOCK, (b + 1) * BLOCK)
        s = jnp.where(times[b] > 0, scores[:, span], F32(-1e30))
        expo = jnp.exp(s - jnp.max(s, axis=0, keepdims=True))
        probs = expo / jnp.sum(expo * times[b], axis=0, keepdims=True)
        other = probs.astype(BF16).astype(F32)
        mine = (probs - F32(1)).astype(BF16).astype(F32)
        g = other * times[b] * livef[:, span] + ohdst[:, span] * (mine - other)
        hi, lo = split2(g)
        his.append(hi)
        los.append(lo)
    ghi = jnp.concatenate(his, axis=1)
    glo = jnp.concatenate(los, axis=1)
    tablet = table.astype(F32).T.astype(BF16)[0:D, :]
    dquery = nn(tablet, ghi) + nn(tablet, glo)
    fbuf[...] = dquery * lhsv[...]

    def rel_half(half):
        hi, lo = split2(fbuf[pl.ds(pl.multiple_of(half * 200, 8), 200), :])
        picks = ohrel[...]
        return nt(hi, picks) + nt(lo, picks)

    rg[...] = rel_half(1 - c)
    cc = [
        send("core", 0, rg.at[0:PART_A, :], crecv.at[0:PART_A, :], to_core),
        send("core", 1, rg.at[PART_A:200, :], crecv.at[PART_A:200, :], to_core),
    ]
    rgs[...] = rel_half(c)

    grads = nt(ghi, query4[...].reshape(512, EDGES)) + nt(glo, query4[...].reshape(512, EDGES))
    for q in range(4):
        tg[q] = grads[:, q * 128 : (q + 1) * 128]

    def lanes(index):
        return pl.ds(pl.multiple_of(index * 128, 128), 128)

    def reduce_first(part, stage, rows, buf, coord, to):
        cc[part].wait_recv()
        rgs[rows, :] = rgs[rows, :] + crecv[rows, :]
        return [
            send(stage, d - 1, rgs.at[rows, lanes(lax.rem(coord + d, NY))], buf.at[d - 1], to(d))
            for d in range(1, NY)
        ]

    rows_a, rows_b = slice(0, PART_A), slice(PART_A, 200)
    cs1a = reduce_first(0, "s1a", rows_a, a1, y, to_y)
    cs1b = reduce_first(1, "s1b", rows_b, b1, z, to_z)

    ctx = [
        send("tx", d - 1, tg.at[lax.rem(x + d, NX)], tgr.at[d - 1], to_x(d)) for d in range(1, NX)
    ]
    hi, lo = split2(dquery * relr[...])
    relr[:, 0:SLOTS] = nt(hi, ohsrc[...]) + nt(lo, ohsrc[...])
    for q in range(4):
        lg[q, 0:QUARTER, :] = relr[q * QUARTER : (q + 1) * QUARTER, 0:SLOTS]
        lg[q, QUARTER:104, :] = jnp.zeros((104 - QUARTER, SLOTS), F32)
    clx = [
        send("lx", d - 1, lg.at[lax.rem(x + d, NX)], lgr.at[d - 1], to_x(d)) for d in range(1, NX)
    ]

    landed(ctx)
    tgs[...] = ((tg[x] + tgr[0]) + (tgr[1] + tgr[2])).reshape(2, 128, 128)
    cry = []
    for d in range(1, NY):
        to = lax.rem(y + d, NY)
        cry.append(send("ry", d - 1, tgs.at[:, y_rows(to), :], ryb.at[:, y_rows(y), :], to_y(d)))
    ryb[:, y_rows(y), :] = tgs[:, y_rows(y), :]

    def reduce_second(copies, stage, rows, buf, coord, total, coord2, buf2, to):
        landed(copies)
        height = rows.stop - rows.start
        summed = rgs[rows, lanes(coord)]
        for d in range(NY - 1):
            summed = summed + buf[d]
        total[0:height, :] = summed
        total[height:128, :] = jnp.zeros((128 - height, 128), F32)
        return [
            send(stage, d - 1, total.at[y_rows(lax.rem(coord2 + d, NY)), :], buf2.at[d - 1], to(d))
            for d in range(1, NY)
        ]

    cs2a = reduce_second(cs1a, "s2a", rows_a, a1, y, a1s, z, a2, to_z)
    cs2b = reduce_second(cs1b, "s2b", rows_b, b1, z, b1s, y, b2, to_y)

    landed(cry)
    hi, lo = split2(ryb[...].reshape(SLOTS, 128))
    both = nn(perm[...], jnp.concatenate([hi, lo], axis=1))
    rzs[...] = both[:, 0:128] + both[:, 128:256]
    crz = []
    for d in range(1, NZC):
        to = lax.rem(zc + d, NZC)
        crz.append(send("rz", d - 1, rzs.at[y_rows(to), :], rzb.at[y_rows(zc), :], to_zc(d)))
    rzb[y_rows(zc), :] = rzs[y_rows(zc), :]

    landed(cs2a)
    landed(cs2b)
    suma, sumb = a1s[y_rows(z), :], b1s[y_rows(y), :]
    for d in range(NY - 1):
        suma, sumb = suma + a2[d], sumb + b2[d]
    s3[x, 0:16, :] = suma
    s3[x, 16:32, :] = sumb
    cs3 = [send("s3", d - 1, s3.at[x], s3.at[x], to_x(d)) for d in range(1, NX)]
    landed(cs3)
    total = ((s3[0] + s3[1]) + (s3[2] + s3[3])).astype(BF16)
    ga[y_rows(z), :] = total[0:16]
    gb[y_rows(y), :] = total[16:32]
    cs4a = [send("s4a", d - 1, ga.at[y_rows(z), :], ga.at[y_rows(z), :], to_z(d)) for d in range(1, NY)]
    cs4b = [send("s4b", d - 1, gb.at[y_rows(y), :], gb.at[y_rows(y), :], to_y(d)) for d in range(1, NY)]

    landed(crz)
    landed(clx)
    hi, lo = split2(rzb[...])
    both = nn(ohsp[...], jnp.concatenate([hi, lo], axis=1))
    added = (both[:, 0:128] + both[:, 128:256]).T
    mine = (lg[x] + lgr[0]) + (lgr[1] + lgr[2])
    out_ent[...] = mine[0:QUARTER, :] + added[0:QUARTER, :]

    base = pl.multiple_of(c * 208, 16)
    span_a, span_b = pl.ds(base, 112), pl.ds(pl.multiple_of(base + 112, 16), 96)
    landed(cs4a)
    cs5a = [
        send("s5a", d - 1, ga.at[0:112, :], gath.at[span_a, lanes(y)], to_y(d)) for d in range(1, NY)
    ]
    gath[span_a, lanes(y)] = ga[0:112, :]
    landed(cs4b)
    cs5b = [
        send("s5b", d - 1, gb.at[0:96, :], gath.at[span_b, lanes(z)], to_z(d)) for d in range(1, NY)
    ]
    gath[span_b, lanes(z)] = gb[0:96, :]
    cs6 = []
    for d in range(NY):
        for k, (copies, span, coord) in enumerate(((cs5a, span_a, y), (cs5b, span_b, z))):
            if d:
                copies[d - 1].wait_recv()
            where = gath.at[span, lanes(lax.rem(coord - d + NY, NY))]
            cs6.append(send("s6", 2 * d + k, where, where, to_core))
    landed(cs6)
    for copy in started:
        copy.wait_send()


def shards(entities, relation, serve_ids, edge_src, edge_rel, edge_dst, neg_ids, edge_count):
    vmem = pl.BlockSpec(memory_space=pltpu.VMEM)
    v = pltpu.VMEM
    scratch = [
        v((D, NREL), F32), v((2, 128, 512), BF16), v((256, 256), BF16), v((2, 128, 256), BF16),
        v((256, 256), BF16), v((256, 256), BF16), v((256, 256), BF16), v((2, 128, 256), BF16),
        v((2, 128, 512), BF16), v((256, 256), BF16), v((256, 256), BF16), v((256, 256), BF16),
        v((SLOTS, EDGES), BF16), v((RELP, EDGES), BF16), v((D, EDGES), F32), v((D, EDGES), F32),
        v((D, EDGES), F32), v((D, EDGES), BF16), v((4, 128, EDGES), BF16),
        v((200, RELP), F32), v((200, RELP), F32), v((200, RELP), F32),
        v((7, PART_A, 128), F32), v((128, 128), F32), v((7, PART_B, 128), F32), v((128, 128), F32),
        v((7, 16, 128), F32), v((7, 16, 128), F32), v((4, 32, 128), F32),
        v((128, 128), BF16), v((128, 128), BF16),
        v((4, 256, 128), F32), v((3, 256, 128), F32), v((2, 128, 128), F32), v((2, 128, 128), F32),
        v((256, 128), F32), v((256, 128), F32), v((4, 104, 256), F32), v((3, 104, 256), F32),
        pltpu.SemaphoreType.DMA, pltpu.SemaphoreType.DMA((COPIES,)), pltpu.SemaphoreType.DMA((COPIES,)),
    ]
    ent_t, gath = pl.pallas_call(
        kernel,
        out_shape=(
            jax.ShapeDtypeStruct((QUARTER, SLOTS), F32),
            jax.ShapeDtypeStruct((416, RELP), BF16),
        ),
        in_specs=[
            vmem, pl.BlockSpec(memory_space=pl.ANY), vmem, vmem, vmem, vmem, vmem,
            pl.BlockSpec(memory_space=pltpu.SMEM),
        ],
        out_specs=(vmem, vmem),
        scratch_shapes=scratch,
        compiler_params=pltpu.CompilerParams(
            collective_id=0, has_side_effects=True, vmem_limit_bytes=48 * 1024 * 1024
        ),
    )(
        entities.T, relation.T, serve_ids[0].T, edge_src[0], edge_rel[0], edge_dst[0],
        neg_ids[0, 0], edge_count,
    )
    summed = jnp.concatenate(
        [gath[0:104], gath[112:208], gath[208:312], gath[320:416]], axis=0
    )[:, 0:NREL].astype(F32)
    slots = EDGES * lax.axis_size("dom") * lax.axis_size("rep")
    return ent_t.T, (summed / F32(slots)).T


def solution(mesh):
    placed = (
        P("dom", None),
        P(),
        P("dom", None, None),
        P("dom", "rep", None),
        P("dom", "rep", None),
        P("dom", "rep", None),
        P("dom", "rep", None, None),
        P("dom", "rep"),
    )
    return jax.shard_map(
        shards, mesh=mesh, in_specs=placed, out_specs=(P("dom", "rep"), P()), check_vma=False
    )
```

```python
import jax
import jax.numpy as jnp
from jax import lax
from jax.experimental import pallas as pl
from jax.experimental.pallas import tpu as pltpu
from jax.sharding import PartitionSpec as P

F32 = jnp.float32
BF16 = jnp.bfloat16
I32 = jnp.int32
NX, NY, NZC = 4, 8, 16
D, NREL, RELP = 400, 1000, 1024
SLOTS, EDGES, BLOCK, GROUPS = 256, 512, 256, 2
QUARTER = 100
PART_A, PART_B = 72, 136
STAGES = (
    "a1", "a2", "b1", "b2", "core0", "core1", "core2", "s1a", "s1b", "s1x", "s2a", "s2b", "s2x",
    "s3", "s3x", "s4a", "s4b", "s4x", "s5a", "s5b", "s5x", "s6", "tx", "lx", "ry", "rz",
)
SINGLY = {"s5a": 0, "s5b": 7, "s5x": 14}
ARRIVALS = len(STAGES) + 17


def nn(a, b):
    return jnp.dot(a, b, preferred_element_type=F32)


def nt(a, b):
    return lax.dot_general(a, b, (((1,), (1,)), ((), ())), preferred_element_type=F32)


def split2(v):
    hi = v.astype(BF16)
    return hi, (v - hi.astype(F32)).astype(BF16)


def onehot(shape, axis, ids):
    return jnp.where(lax.broadcasted_iota(I32, shape, axis) == ids, F32(1), F32(0))


def kernel(
    ent_hbm, rel_hbm, serve_hbm, src_hbm, rel_ids_hbm, dst_hbm, neg_hbm, count,
    out_ent, gath,
    ent, serve, src, rel, dst, neg, relv, outs, outp, ra1, ra1p, ra2, rb1, rb1p, tab, perm, permt, ohsp,
    ohsrc, ohrel, fbuf, lhsv, relr, query, query4,
    rg, crecv, rgs, a1, a1s, b1, b1s, x1, x1s, a2, b2, x2, s3, x3, ga, gb, gx,
    tg, tgr, tgs, ryb, rzs, rzb, lg, lgr,
    insem, ssem, rsem,
):
    me, x = lax.axis_index("dom"), lax.axis_index("rep")
    y, zc = me // NZC, lax.rem(me, NZC)
    z, c = zc // 2, lax.rem(zc, 2)

    def to_y(d):
        return {"dom": lax.rem(y + d, NY) * NZC + zc, "rep": x}

    def to_zc(d):
        return {"dom": y * NZC + lax.rem(zc + d, NZC), "rep": x}

    def to_z(d):
        return {"dom": y * NZC + lax.rem(z + d, NY) * 2 + c, "rep": x}

    def to_x(d):
        return {"dom": me, "rep": lax.rem(x + d, NX)}

    to_core = {"dom": y * NZC + z * 2 + 1 - c, "rep": x}
    whole = {
        "a1": ra1.at[:, 0:112, :], "a2": ra2.at[0:240, :],
        "b1": rb1.at[0:240, :], "b2": tab.at[:, 0:112, 256:512],
        "core0": crecv.at[0:PART_A, :], "core1": crecv.at[PART_A:PART_B, :],
        "core2": crecv.at[PART_B:200, :],
        "s1a": a1, "s1b": b1, "s1x": x1, "s2a": a2, "s2b": b2, "s2x": x2,
        "s3": s3.at[0:3], "s3x": x3.at[0:7],
        "s4a": ga.at[0:112, :], "s4b": gb.at[0:112, :], "s4x": ga.at[0:112, :],
        "s5a": gath.at[0:80, 0:896], "s5b": gath.at[0:64, 0:896], "s5x": gath.at[0:64, 0:768],
        "s6": gath.at[0:208, :], "tx": tgr, "lx": lgr,
        "ry": ryb.at[:, 0:112, :], "rz": rzb.at[0:240, :],
    }

    def send(stage, i, source, target, device):
        n = STAGES.index(stage)
        arrival = len(STAGES) + SINGLY[stage] + i if stage in SINGLY else n
        copy = pltpu.make_async_remote_copy(
            src_ref=source, dst_ref=target, send_sem=ssem.at[n], recv_sem=rsem.at[arrival],
            device_id=device, device_id_type=pl.DeviceIdType.MESH,
        )
        copy.start()
        return copy

    def landed(stage):
        pltpu.make_async_copy(whole[stage], whole[stage], rsem.at[STAGES.index(stage)]).wait()

    fetches = []
    for n, (source, target) in enumerate((
        (ent_hbm, ent), (serve_hbm, serve), (src_hbm, src), (rel_ids_hbm, rel),
        (rel_hbm, relv), (dst_hbm, dst), (neg_hbm, neg),
    )):
        fetches.append(pltpu.make_async_copy(source, target, insem.at[n]))
        fetches[n].start()

    barrier = pltpu.get_barrier_semaphore()
    partners = [to_y(d) for d in range(1, NY)] + [to_zc(d) for d in range(1, NZC)]
    partners += [to_x(d) for d in range(1, NX)]
    for device in partners:
        pl.semaphore_signal(barrier, inc=1, device_id=device, device_id_type=pl.DeviceIdType.MESH)

    row = lax.broadcasted_iota(I32, (SLOTS, SLOTS), 0)
    col = lax.broadcasted_iota(I32, (SLOTS, SLOTS), 1)
    moved = lax.rem(col, 16) * 16 + (col // 128) * 8 + lax.rem(col // 16, 8)
    perm[...] = jnp.where(row == moved, F32(1), F32(0)).astype(BF16)
    moved = lax.rem(row, 16) * 16 + (row // 128) * 8 + lax.rem(row // 16, 8)
    permt[...] = jnp.where(col == moved, F32(1), F32(0)).astype(BF16)
    fetches[1].wait()
    served = jnp.concatenate([serve[0:1, :], serve[1:2, :]], axis=1)
    ohst = jnp.where(row == served, F32(1), F32(0))
    ohs = ohst.T.astype(BF16)
    fetches[0].wait()
    outs[:, :, 384:512] = jnp.zeros((2, 128, 128), BF16)
    outs[:, :, 0:D] = nt(ohs, ent[...]).astype(BF16).reshape(2, 128, D)
    outp[:, 128:256] = jnp.zeros((SLOTS, 128), BF16)
    outp[:, 0 : D - 256] = nn(perm[...], outs[:, :, 256:D].reshape(SLOTS, D - 256)).astype(BF16)

    pl.semaphore_wait(barrier, len(partners))

    def y_rows(index):
        return pl.ds(pl.multiple_of(index * 16, 16), 16)

    for d in range(1, NY):
        to = lax.rem(y + d, NY)
        send("a1", d - 1, outs.at[:, y_rows(to), 0:256], ra1.at[:, y_rows(y), :], to_y(d))
    for d in range(1, NZC):
        to = lax.rem(zc + d, NZC)
        send("b1", d - 1, outp.at[y_rows(to), :], rb1.at[y_rows(zc), :], to_zc(d))
    ra1[:, y_rows(y), :] = outs[:, y_rows(y), 0:256]
    rb1[y_rows(zc), :] = outp[y_rows(zc), :]

    ohsp[...] = nt(ohst.astype(BF16), perm[...]).astype(BF16)
    fetches[2].wait()
    ohsrc[...] = onehot((SLOTS, EDGES), 0, src[...]).astype(BF16)
    fbuf[...] = nn(ent[...], ohsrc[...])
    lhsv[...] = fbuf[...]
    fetches[3].wait()
    ohrel[...] = onehot((RELP, EDGES), 0, rel[...]).astype(BF16)
    fetches[4].wait()
    for q in range(4):
        part = relv[q * 104 : min(D, q * 104 + 104), :]
        hi = part.astype(BF16)
        rest = part - hi.astype(F32)
        mid = rest.astype(BF16)
        low = (rest - mid.astype(F32)).astype(BF16)
        picks = ohrel[0:NREL, :]
        relr[q * 104 : min(D, q * 104 + 104), :] = (nn(hi, picks) + nn(mid, picks)) + nn(low, picks)
    fbuf[...] = lhsv[...] * relr[...]
    query[...] = fbuf[...].astype(BF16)
    query4[...] = jnp.zeros(query4.shape, BF16)
    for q in range(4):
        query4[q, 0:QUARTER, :] = fbuf[q * QUARTER : (q + 1) * QUARTER, :].astype(BF16)

    for n in (5, 6):
        fetches[n].wait()
    live = lax.broadcasted_iota(I32, (1, EDGES), 1) < count[0, 0]
    livef = jnp.where(live, F32(1), F32(0))
    dsts = lax.rem(dst[...], 2) * 128 + dst[...] // 2
    negs = lax.rem(neg[...], 2) * 128 + neg[...] // 2
    ohdst = onehot((SLOTS, EDGES), 0, dsts) * livef
    times = []
    for b in range(GROUPS):
        ohneg = onehot((SLOTS, negs.shape[1]), 0, negs[b : b + 1, :])
        own = ohdst[:, b * BLOCK : (b + 1) * BLOCK]
        times.append(
            jnp.sum(ohneg, axis=1, keepdims=True) + jnp.sum(own, axis=1, keepdims=True)
        )

    landed("a1")
    ra1p[...] = nn(perm[...], ra1[...].reshape(SLOTS, 256)).astype(BF16)
    for d in range(1, NZC):
        to = lax.rem(zc + d, NZC)
        send("a2", d - 1, ra1p.at[y_rows(to), :], ra2.at[y_rows(zc), :], to_zc(d))
    ra2[y_rows(zc), :] = ra1p[y_rows(zc), :]
    landed("b1")
    rb1p[...] = nn(permt[...], rb1[...]).astype(BF16).reshape(2, 128, 256)
    for d in range(1, NY):
        to = lax.rem(y + d, NY)
        send("b2", d - 1, rb1p.at[:, y_rows(to), :], tab.at[:, y_rows(y), 256:512], to_y(d))
    tab[:, y_rows(y), 256:512] = rb1p[:, y_rows(y), :]
    landed("a2")
    tab[:, :, 0:256] = nn(permt[...], ra2[...]).astype(BF16).reshape(2, 128, 256)
    landed("b2")

    table = tab[...].reshape(SLOTS, 512)
    scores = nn(table[:, 0:D], query[...])
    his, los = [], []
    for b in range(GROUPS):
        span = slice(b * BLOCK, (b + 1) * BLOCK)
        s = jnp.where(times[b] > 0, scores[:, span], F32(-1e30))
        expo = jnp.exp(s - jnp.max(s, axis=0, keepdims=True))
        probs = expo / jnp.sum(expo * times[b], axis=0, keepdims=True)
        other = probs.astype(BF16).astype(F32)
        mine = (probs - F32(1)).astype(BF16).astype(F32)
        g = other * times[b] * livef[:, span] + ohdst[:, span] * (mine - other)
        hi, lo = split2(g)
        his.append(hi)
        los.append(lo)
    ghi = jnp.concatenate(his, axis=1)
    glo = jnp.concatenate(los, axis=1)
    tablet = table.astype(F32).T.astype(BF16)[0:D, :]
    dquery = nn(tablet, ghi) + nn(tablet, glo)
    fbuf[...] = dquery * lhsv[...]

    def rel_half(half):
        hi, lo = split2(fbuf[pl.ds(pl.multiple_of(half * 200, 8), 200), :])
        picks = ohrel[...]
        return nt(hi, picks) + nt(lo, picks)

    rows_a, rows_b, rows_x = slice(0, PART_A), slice(PART_A, PART_B), slice(PART_B, 200)
    rg[...] = rel_half(1 - c)
    for n, rows in enumerate((rows_a, rows_b, rows_x)):
        send("core%d" % n, 0, rg.at[rows, :], crecv.at[rows, :], to_core)
    rgs[...] = rel_half(c)

    grads = nt(ghi, query4[...].reshape(512, EDGES)) + nt(glo, query4[...].reshape(512, EDGES))
    for q in range(4):
        tg[q] = grads[:, q * 128 : (q + 1) * 128]

    def lanes(index, width=128):
        return pl.ds(pl.multiple_of(index * width, 128), width)

    def reduce_first(part, stage, rows, buf, coord, size, to):
        landed("core%d" % part)
        rgs[rows, :] = rgs[rows, :] + crecv[rows, :]
        width = RELP // size
        for d in range(1, size):
            source = rgs.at[rows, lanes(lax.rem(coord + d, size), width)]
            send(stage, d - 1, source, buf.at[d - 1], to(d))

    reduce_first(0, "s1a", rows_a, a1, y, NY, to_y)
    reduce_first(1, "s1b", rows_b, b1, z, NY, to_z)
    reduce_first(2, "s1x", rows_x, x1, x, NX, to_x)
    for d in range(1, NX):
        send("tx", d - 1, tg.at[lax.rem(x + d, NX)], tgr.at[d - 1], to_x(d))
    hi, lo = split2(dquery * relr[...])
    relr[:, 0:SLOTS] = nt(hi, ohsrc[...]) + nt(lo, ohsrc[...])
    for q in range(4):
        lg[q, 0:QUARTER, :] = relr[q * QUARTER : (q + 1) * QUARTER, 0:SLOTS]
        lg[q, QUARTER:104, :] = jnp.zeros((104 - QUARTER, SLOTS), F32)

    def tile_of(index):
        return y_rows(lax.rem(index, 4)), lanes(index // 4)

    landed("s1x")
    x1s[...] = (rgs[rows_x, lanes(x, 256)] + x1[0]) + (x1[1] + x1[2])
    for d in range(1, NY):
        send("s2x", d - 1, x1s.at[tile_of(lax.rem(y + d, NY))], x2.at[d - 1], to_y(d))

    def reduce_second(first, stage, rows, buf, coord, total, coord2, buf2, to):
        landed(first)
        height = rows.stop - rows.start
        summed = rgs[rows, lanes(coord)]
        for d in range(NY - 1):
            summed = summed + buf[d]
        total[0:height, :] = summed
        total[height:128, :] = jnp.zeros((128 - height, 128), F32)
        for d in range(1, NY):
            source = total.at[y_rows(lax.rem(coord2 + d, NY)), :]
            send(stage, d - 1, source, buf2.at[d - 1], to(d))

    reduce_second("s1a", "s2a", rows_a, a1, y, a1s, z, a2, to_z)
    reduce_second("s1b", "s2b", rows_b, b1, z, b1s, y, b2, to_y)

    landed("tx")
    tgs[...] = ((tg[x] + tgr[0]) + (tgr[1] + tgr[2])).astype(BF16).reshape(2, 128, 128)
    for d in range(1, NY):
        to = lax.rem(y + d, NY)
        send("ry", d - 1, tgs.at[:, y_rows(to), :], ryb.at[:, y_rows(y), :], to_y(d))
    ryb[:, y_rows(y), :] = tgs[:, y_rows(y), :]

    landed("s2x")
    sumx = x1s[tile_of(y)]
    for d in range(NY - 1):
        sumx = sumx + x2[d]
    x3[z] = sumx
    for d in range(1, NY):
        send("s3x", d - 1, x3.at[z], x3.at[z], to_z(d))

    landed("s2a")
    landed("s2b")
    suma, sumb = a1s[y_rows(z), :], b1s[y_rows(y), :]
    for d in range(NY - 1):
        suma, sumb = suma + a2[d], sumb + b2[d]
    s3[x, 0:16, :] = suma
    s3[x, 16:32, :] = sumb
    for d in range(1, NX):
        send("s3", d - 1, s3.at[x], s3.at[x], to_x(d))
    for d in range(1, NX):
        send("lx", d - 1, lg.at[lax.rem(x + d, NX)], lgr.at[d - 1], to_x(d))

    landed("ry")
    rzs[...] = nn(perm[...], ryb[...].reshape(SLOTS, 128)).astype(BF16)

    landed("s3")
    total = ((s3[0] + s3[1]) + (s3[2] + s3[3])).astype(BF16)
    ga[y_rows(z), :] = total[0:16]
    gb[y_rows(y), :] = total[16:32]
    for d in range(1, NY):
        send("s4a", d - 1, ga.at[y_rows(z), :], ga.at[y_rows(z), :], to_z(d))
    for d in range(1, NY):
        send("s4b", d - 1, gb.at[y_rows(y), :], gb.at[y_rows(y), :], to_y(d))
    landed("s3x")
    total = ((x3[0] + x3[1]) + (x3[2] + x3[3])) + ((x3[4] + x3[5]) + (x3[6] + x3[7]))
    gx[tile_of(y)] = total.astype(BF16)
    for d in range(1, NY):
        send("s4x", d - 1, gx.at[tile_of(y)], gx.at[tile_of(y)], to_y(d))
    for d in range(1, NZC):
        to = lax.rem(zc + d, NZC)
        send("rz", d - 1, rzs.at[y_rows(to), :], rzb.at[y_rows(zc), :], to_zc(d))
    rzb[y_rows(zc), :] = rzs[y_rows(zc), :]

    base = c * 208
    span_a = pl.ds(pl.multiple_of(base, 16), 80)
    span_b = pl.ds(pl.multiple_of(base + 80, 16), 64)
    span_x = pl.ds(pl.multiple_of(base + 144, 16), 64)
    landed("s4a")
    cs5a = [
        send("s5a", d - 1, ga.at[0:80, :], gath.at[span_a, lanes(y)], to_y(d)) for d in range(1, NY)
    ]
    gath[span_a, lanes(y)] = ga[0:80, :]
    landed("s4b")
    cs5b = [
        send("s5b", d - 1, gb.at[0:64, :], gath.at[span_b, lanes(z)], to_z(d)) for d in range(1, NY)
    ]
    gath[span_b, lanes(z)] = gb[0:64, :]
    landed("s4x")
    cs5x = [
        send("s5x", d - 1, gx, gath.at[span_x, lanes(x, 256)], to_x(d)) for d in range(1, NX)
    ]
    gath[span_x, lanes(x, 256)] = gx[...]

    landed("rz")
    landed("lx")
    added = nn(ohsp[...], rzb[...]).T
    mine = (lg[x] + lgr[0]) + (lgr[1] + lgr[2])
    out_ent[...] = mine[0:QUARTER, :] + added[0:QUARTER, :]

    pieces = [0]

    def forward(copies, d, span, coord, size):
        if d:
            copies[d - 1].wait_recv()
        where = gath.at[span, lanes(lax.rem(coord - d + size, size), RELP // size)]
        send("s6", pieces[0], where, where, to_core)
        pieces[0] += 1

    for d in range(NY):
        forward(cs5a, d, span_a, y, NY)
        forward(cs5b, d, span_b, z, NY)
        if d < NX:
            forward(cs5x, d, span_x, x, NX)
    landed("s6")
    for n, stage in enumerate(STAGES):
        pltpu.make_async_copy(whole[stage], whole[stage], ssem.at[n]).wait()


def shards(entities, relation, serve_ids, edge_src, edge_rel, edge_dst, neg_ids, edge_count):
    vmem = pl.BlockSpec(memory_space=pltpu.VMEM)
    v = pltpu.VMEM
    scratch = [
        v((D, SLOTS), BF16), v((2, 128), I32), v((1, EDGES), I32), v((1, EDGES), I32),
        v((1, EDGES), I32), v((2, 384), I32),
        v((D, NREL), F32), v((2, 128, 512), BF16), v((256, 256), BF16), v((2, 128, 256), BF16),
        v((256, 256), BF16), v((256, 256), BF16), v((256, 256), BF16), v((2, 128, 256), BF16),
        v((2, 128, 512), BF16), v((256, 256), BF16), v((256, 256), BF16), v((256, 256), BF16),
        v((SLOTS, EDGES), BF16), v((RELP, EDGES), BF16), v((D, EDGES), F32), v((D, EDGES), F32),
        v((D, EDGES), F32), v((D, EDGES), BF16), v((4, 128, EDGES), BF16),
        v((200, RELP), F32), v((200, RELP), F32), v((200, RELP), F32),
        v((7, 72, 128), F32), v((128, 128), F32), v((7, 64, 128), F32), v((128, 128), F32),
        v((3, 64, 256), F32), v((64, 256), F32),
        v((7, 16, 128), F32), v((7, 16, 128), F32), v((7, 16, 128), F32),
        v((4, 32, 128), F32), v((8, 16, 128), F32),
        v((128, 128), BF16), v((128, 128), BF16), v((64, 256), BF16),
        v((4, 256, 128), F32), v((3, 256, 128), F32), v((2, 128, 128), BF16), v((2, 128, 128), BF16),
        v((256, 128), BF16), v((256, 128), BF16), v((4, 104, 256), F32), v((3, 104, 256), F32),
        pltpu.SemaphoreType.DMA((7,)), pltpu.SemaphoreType.DMA((len(STAGES),)), pltpu.SemaphoreType.DMA((ARRIVALS,)),
    ]
    operands = (
        entities.T, relation.T, serve_ids[0].T, edge_src[0], edge_rel[0], edge_dst[0],
        neg_ids[0, 0],
    )
    ent_t, gath = pl.pallas_call(
        kernel,
        out_shape=(
            jax.ShapeDtypeStruct((QUARTER, SLOTS), F32),
            jax.ShapeDtypeStruct((416, RELP), BF16),
        ),
        in_specs=[pl.BlockSpec(memory_space=pltpu.HBM)] * 7 + [pl.BlockSpec(memory_space=pltpu.SMEM)],
        out_specs=(vmem, vmem),
        scratch_shapes=scratch,
        compiler_params=pltpu.CompilerParams(
            collective_id=0, has_side_effects=True, vmem_limit_bytes=48 * 1024 * 1024
        ),
    )(
        *(pltpu.with_memory_space_constraint(a, pltpu.HBM) for a in operands), edge_count
    )
    summed = jnp.concatenate(
        [gath[0:72], gath[80:280], gath[288:416]], axis=0
    )[:, 0:NREL].astype(F32)
    slots = EDGES * lax.axis_size("dom") * lax.axis_size("rep")
    return ent_t.T, (summed / F32(slots)).T


def solution(mesh):
    placed = (
        P("dom", None),
        P(),
        P("dom", None, None),
        P("dom", "rep", None),
        P("dom", "rep", None),
        P("dom", "rep", None),
        P("dom", "rep", None, None),
        P("dom", "rep"),
    )
    return jax.shard_map(
        shards, mesh=mesh, in_specs=placed, out_specs=(P("dom", "rep"), P()), check_vma=False
    )
```

```python
import functools

import jax
import jax.numpy as jnp
from jax import lax
from jax.experimental import pallas as pl
from jax.experimental.pallas import tpu as pltpu
from jax.sharding import PartitionSpec as P

F32 = jnp.float32
BF16 = jnp.bfloat16
I32 = jnp.int32
NX, NY, NZC = 4, 8, 16
FAR_X, FAR_Y = (2, 1, 3), (4, 3, 5, 2, 6, 1, 7)
FAR_ZC = (8, 7, 9, 6, 10, 5, 11, 4, 12, 3, 13, 2, 14, 1, 15)
D, NREL, RELP = 400, 1000, 1024
SLOTS, EDGES, BLOCK, GROUPS = 256, 512, 256, 2
QUARTER = 100
PART_A, PART_B = 56, 104
STAGES = (
    "a1", "a2", "b1", "b2", "core0", "core1", "core2", "s1a", "s1b", "s1x", "s2a", "s2b", "s2x",
    "s3a", "s3b", "s3x", "s4a", "s4b", "s4x", "s5a", "s5b", "s5x", "s6", "tx", "lx", "ry", "rz",
)
SINGLY = {"s5a": 0, "s5b": 7, "s5x": 14}
ARRIVALS = len(STAGES) + 17


def nn(a, b):
    return jnp.dot(a, b, preferred_element_type=F32)


def nt(a, b):
    return lax.dot_general(a, b, (((1,), (1,)), ((), ())), preferred_element_type=F32)


def split2(v):
    hi = v.astype(BF16)
    return hi, (v - hi.astype(F32)).astype(BF16)


def onehot(shape, axis, ids):
    return jnp.where(lax.broadcasted_iota(I32, shape, axis) == ids, F32(1), F32(0))


def kernel(
    ent_hbm, rel_hbm, serve_hbm, src_hbm, rel_ids_hbm, dst_hbm, neg_hbm, count,
    out_ent, gath,
    ent, serve, src, rel, dst, neg, relv, outs, outp, ra1, ra1p, ra2, rb1, rb1p, tab, perm, permt, ohsp,
    ohsrc, ohrel, fbuf, lhsv, relr, query, query4,
    rg, crecv, rgs, a1, a1s, b1, b1s, x1, x1s, a2, b2, x2, a3, b3, x3, ga, gb, gx8, gx,
    tg, tgr, tgs, ryb, rzs, rzb, lg, lgr,
    insem, ssem, rsem,
):
    me, x = lax.axis_index("dom"), lax.axis_index("rep")
    y, zc = me // NZC, lax.rem(me, NZC)
    z, c = zc // 2, lax.rem(zc, 2)

    def to_y(d):
        return {"dom": lax.rem(y + d, NY) * NZC + zc, "rep": x}

    def to_zc(d):
        return {"dom": y * NZC + lax.rem(zc + d, NZC), "rep": x}

    def to_z(d):
        return {"dom": y * NZC + lax.rem(z + d, NY) * 2 + c, "rep": x}

    def to_x(d):
        return {"dom": me, "rep": lax.rem(x + d, NX)}

    to_core = {"dom": y * NZC + z * 2 + 1 - c, "rep": x}
    whole = {
        "a1": ra1.at[:, 0:112, :], "a2": ra2.at[0:240, :],
        "b1": rb1.at[0:240, :], "b2": tab.at[:, 0:112, 256:512],
        "core0": crecv.at[0:PART_A, :], "core1": crecv.at[PART_A:PART_B, :],
        "core2": crecv.at[PART_B:200, :],
        "s1a": a1, "s1b": b1, "s1x": x1, "s2a": a2, "s2b": b2, "s2x": x2,
        "s3a": a3.at[0:7], "s3b": b3.at[0:7], "s3x": x3.at[0:7],
        "s4a": ga.at[0:48, :], "s4b": gb.at[0:48, :], "s4x": gx8.at[0:7],
        "s5a": gath.at[0:64, 0:896], "s5b": gath.at[0:48, 0:896], "s5x": gath.at[0:96, 0:768],
        "s6": gath.at[0:208, :], "tx": tgr, "lx": lgr,
        "ry": ryb.at[:, 0:112, :], "rz": rzb.at[0:240, :],
    }

    def send(stage, i, source, target, device):
        n = STAGES.index(stage)
        arrival = len(STAGES) + SINGLY[stage] + i if stage in SINGLY else n
        copy = pltpu.make_async_remote_copy(
            src_ref=source, dst_ref=target, send_sem=ssem.at[n], recv_sem=rsem.at[arrival],
            device_id=device, device_id_type=pl.DeviceIdType.MESH,
        )
        copy.start()
        return copy

    def landed(stage):
        pltpu.make_async_copy(whole[stage], whole[stage], rsem.at[STAGES.index(stage)]).wait()

    barrier = pltpu.get_barrier_semaphore()
    partners = [to_y(d) for d in FAR_Y] + [to_zc(d) for d in FAR_ZC]
    partners += [to_x(d) for d in FAR_X]
    for device in partners:
        pl.semaphore_signal(barrier, inc=1, device_id=device, device_id_type=pl.DeviceIdType.MESH)

    fetches = []
    for n, (source, target) in enumerate((
        (ent_hbm, ent), (serve_hbm, serve), (src_hbm, src), (rel_ids_hbm, rel),
        (rel_hbm, relv), (dst_hbm, dst), (neg_hbm, neg),
    )):
        fetches.append(pltpu.make_async_copy(source, target, insem.at[n]))
        fetches[n].start()

    row = lax.broadcasted_iota(I32, (SLOTS, SLOTS), 0)
    col = lax.broadcasted_iota(I32, (SLOTS, SLOTS), 1)
    moved = ((col & 15) << 4) + ((col >> 7) << 3) + ((col >> 4) & 7)
    perm[...] = jnp.where(row == moved, F32(1), F32(0)).astype(BF16)
    fetches[1].wait()
    served = jnp.concatenate([serve[0:1, :], serve[1:2, :]], axis=1)
    ohst = jnp.where(row == served, F32(1), F32(0))
    ohs = ohst.T.astype(BF16)
    fetches[0].wait()
    outs[:, :, 384:512] = jnp.zeros((2, 128, 128), BF16)
    outs[:, :, 0:D] = nt(ohs, ent[...]).astype(BF16).reshape(2, 128, D)
    outp[:, 128:256] = jnp.zeros((SLOTS, 128), BF16)
    outp[:, 0 : D - 256] = nn(perm[...], outs[:, :, 256:D].reshape(SLOTS, D - 256)).astype(BF16)

    pl.semaphore_wait(barrier, len(partners))

    def y_rows(index):
        return pl.ds(pl.multiple_of(index * 16, 16), 16)

    for d in FAR_Y:
        to = lax.rem(y + d, NY)
        send("a1", d - 1, outs.at[:, y_rows(to), 0:256], ra1.at[:, y_rows(y), :], to_y(d))
    for d in FAR_ZC:
        to = lax.rem(zc + d, NZC)
        send("b1", d - 1, outp.at[y_rows(to), :], rb1.at[y_rows(zc), :], to_zc(d))
    ra1[:, y_rows(y), :] = outs[:, y_rows(y), 0:256]
    rb1[y_rows(zc), :] = outp[y_rows(zc), :]

    moved = ((row & 15) << 4) + ((row >> 7) << 3) + ((row >> 4) & 7)
    permt[...] = jnp.where(col == moved, F32(1), F32(0)).astype(BF16)
    ohsp[...] = nt(ohst.astype(BF16), perm[...]).astype(BF16)
    fetches[2].wait()
    ohsrc[...] = onehot((SLOTS, EDGES), 0, src[...]).astype(BF16)
    fbuf[...] = nn(ent[...], ohsrc[...])
    lhsv[...] = fbuf[...]
    fetches[3].wait()
    ohrel[...] = onehot((RELP, EDGES), 0, rel[...]).astype(BF16)
    fetches[4].wait()
    for q in range(4):
        part = relv[q * 104 : min(D, q * 104 + 104), :]
        hi = part.astype(BF16)
        rest = part - hi.astype(F32)
        mid = rest.astype(BF16)
        low = (rest - mid.astype(F32)).astype(BF16)
        picks = ohrel[0:NREL, :]
        relr[q * 104 : min(D, q * 104 + 104), :] = (nn(hi, picks) + nn(mid, picks)) + nn(low, picks)
    fbuf[...] = lhsv[...] * relr[...]
    query[...] = fbuf[...].astype(BF16)
    query4[...] = jnp.zeros(query4.shape, BF16)
    for q in range(4):
        query4[q, 0:QUARTER, :] = fbuf[q * QUARTER : (q + 1) * QUARTER, :].astype(BF16)

    for n in (5, 6):
        fetches[n].wait()
    live = lax.broadcasted_iota(I32, (1, EDGES), 1) < count[0, 0]
    livef = jnp.where(live, F32(1), F32(0))
    dsts = ((dst[...] & 1) << 7) + (dst[...] >> 1)
    negs = ((neg[...] & 1) << 7) + (neg[...] >> 1)
    ohdst = onehot((SLOTS, EDGES), 0, dsts) * livef
    times = []
    for b in range(GROUPS):
        ohneg = onehot((SLOTS, negs.shape[1]), 0, negs[b : b + 1, :])
        own = ohdst[:, b * BLOCK : (b + 1) * BLOCK]
        times.append(
            jnp.sum(ohneg, axis=1, keepdims=True) + jnp.sum(own, axis=1, keepdims=True)
        )

    landed("a1")
    ra1p[...] = nn(perm[...], ra1[...].reshape(SLOTS, 256)).astype(BF16)
    for d in FAR_ZC:
        to = lax.rem(zc + d, NZC)
        send("a2", d - 1, ra1p.at[y_rows(to), :], ra2.at[y_rows(zc), :], to_zc(d))
    ra2[y_rows(zc), :] = ra1p[y_rows(zc), :]
    landed("b1")
    rb1p[...] = nn(permt[...], rb1[...]).astype(BF16).reshape(2, 128, 256)
    for d in FAR_Y:
        to = lax.rem(y + d, NY)
        send("b2", d - 1, rb1p.at[:, y_rows(to), :], tab.at[:, y_rows(y), 256:512], to_y(d))
    tab[:, y_rows(y), 256:512] = rb1p[:, y_rows(y), :]
    landed("a2")
    tab[:, :, 0:256] = nn(permt[...], ra2[...]).astype(BF16).reshape(2, 128, 256)
    landed("b2")

    table = tab[...].reshape(SLOTS, 512)
    scores = nn(table[:, 0:D], query[...])
    his, los = [], []
    for b in range(GROUPS):
        span = slice(b * BLOCK, (b + 1) * BLOCK)
        s = jnp.where(times[b] > 0, scores[:, span], F32(-1e30))
        expo = jnp.exp(s - jnp.max(s, axis=0, keepdims=True))
        probs = expo / jnp.sum(expo * times[b], axis=0, keepdims=True)
        other = probs.astype(BF16).astype(F32)
        mine = (probs - F32(1)).astype(BF16).astype(F32)
        g = other * times[b] * livef[:, span] + ohdst[:, span] * (mine - other)
        hi, lo = split2(g)
        his.append(hi)
        los.append(lo)
    ghi = jnp.concatenate(his, axis=1)
    glo = jnp.concatenate(los, axis=1)
    tablet = table.astype(F32).T.astype(BF16)[0:D, :]
    dquery = nn(tablet, ghi) + nn(tablet, glo)
    fbuf[...] = dquery * lhsv[...]

    def rel_half(half):
        hi, lo = split2(fbuf[pl.ds(pl.multiple_of(half * 200, 8), 200), :])
        picks = ohrel[...]
        return nt(hi, picks) + nt(lo, picks)

    rows_a, rows_b, rows_x = slice(0, PART_A), slice(PART_A, PART_B), slice(PART_B, 200)
    rg[...] = rel_half(1 - c)
    for n, rows in enumerate((rows_a, rows_b, rows_x)):
        send("core%d" % n, 0, rg.at[rows, :], crecv.at[rows, :], to_core)
    rgs[...] = rel_half(c)

    grads = nt(ghi, query4[...].reshape(512, EDGES)) + nt(glo, query4[...].reshape(512, EDGES))
    for q in range(4):
        tg[q] = grads[:, q * 128 : (q + 1) * 128]

    def lanes(index, width=128):
        return pl.ds(pl.multiple_of(index * width, 128), width)

    def reduce_first(part, stage, rows, buf, coord, size, to):
        landed("core%d" % part)
        rgs[rows, :] = rgs[rows, :] + crecv[rows, :]
        width = RELP // size
        for d in FAR_X if size == NX else FAR_Y:
            source = rgs.at[rows, lanes(lax.rem(coord + d, size), width)]
            send(stage, d - 1, source, buf.at[d - 1], to(d))

    reduce_first(0, "s1a", rows_a, a1, y, NY, to_y)
    reduce_first(1, "s1b", rows_b, b1, z, NY, to_z)
    reduce_first(2, "s1x", rows_x, x1, x, NX, to_x)
    hi, lo = split2(dquery * relr[...])
    relr[:, 0:SLOTS] = nt(hi, ohsrc[...]) + nt(lo, ohsrc[...])
    for q in range(4):
        lg[q, 0:QUARTER, :] = relr[q * QUARTER : (q + 1) * QUARTER, 0:SLOTS]
        lg[q, QUARTER:104, :] = jnp.zeros((104 - QUARTER, SLOTS), F32)

    def tile_of(index):
        group = pl.multiple_of(lax.rem(index, 4) * 24, 8)
        return pl.ds(group, 24), lanes(index // 4)

    landed("s1x")
    x1s[...] = (rgs[rows_x, lanes(x, 256)] + x1[0]) + (x1[1] + x1[2])
    for d in FAR_Y:
        send("s2x", d - 1, x1s.at[tile_of(lax.rem(y + d, NY))], x2.at[d - 1], to_y(d))

    def reduce_second(first, stage, rows, buf, coord, total, buf2):
        landed(first)
        height = rows.stop - rows.start
        summed = rgs[rows, lanes(coord)]
        for d in range(NY - 1):
            summed = summed + buf[d]
        total[0:height, :] = summed
        total[height:64, :] = jnp.zeros((64 - height, 128), F32)
        for d in FAR_X:
            send(stage, d - 1, total.at[y_rows(lax.rem(x + d, NX)), :], buf2.at[d - 1], to_x(d))

    reduce_second("s1a", "s2a", rows_a, a1, y, a1s, a2)
    reduce_second("s1b", "s2b", rows_b, b1, z, b1s, b2)
    for d in FAR_X:
        send("tx", d - 1, tg.at[lax.rem(x + d, NX)], tgr.at[d - 1], to_x(d))

    def reduce_third(second, stage, total, buf2, buf3, coord, to):
        landed(second)
        buf3[coord] = (total[y_rows(x), :] + buf2[0]) + (buf2[1] + buf2[2])
        for d in FAR_Y:
            send(stage, d - 1, buf3.at[coord], buf3.at[coord], to(d))

    reduce_third("s2a", "s3a", a1s, a2, a3, z, to_z)
    reduce_third("s2b", "s3b", b1s, b2, b3, y, to_y)

    landed("s2x")
    sumx = x1s[tile_of(y)]
    for d in range(NY - 1):
        sumx = sumx + x2[d]
    x3[z] = sumx
    for d in FAR_Y:
        send("s3x", d - 1, x3.at[z], x3.at[z], to_z(d))

    landed("tx")
    tgs[...] = ((tg[x] + tgr[0]) + (tgr[1] + tgr[2])).astype(BF16).reshape(2, 128, 128)
    for d in FAR_Y:
        to = lax.rem(y + d, NY)
        send("ry", d - 1, tgs.at[:, y_rows(to), :], ryb.at[:, y_rows(y), :], to_y(d))
    ryb[:, y_rows(y), :] = tgs[:, y_rows(y), :]

    def sum8(buf):
        return ((buf[0] + buf[1]) + (buf[2] + buf[3])) + ((buf[4] + buf[5]) + (buf[6] + buf[7]))

    def gather_first(third, stage, buf3, buf):
        landed(third)
        buf[y_rows(x), :] = sum8(buf3).astype(BF16)
        for d in FAR_X:
            send(stage, d - 1, buf.at[y_rows(x), :], buf.at[y_rows(x), :], to_x(d))

    gather_first("s3a", "s4a", a3, ga)
    gather_first("s3b", "s4b", b3, gb)
    for d in FAR_X:
        send("lx", d - 1, lg.at[lax.rem(x + d, NX)], lgr.at[d - 1], to_x(d))
    landed("s3x")
    gx8[y, 0:24, :] = sum8(x3).astype(BF16)
    gx8[y, 24:32, :] = jnp.zeros((8, 128), BF16)
    for d in FAR_Y:
        send("s4x", d - 1, gx8.at[y], gx8.at[y], to_y(d))

    base = c * 208
    span_a = pl.ds(pl.multiple_of(base, 16), 64)
    span_b = pl.ds(pl.multiple_of(base + 64, 16), 48)
    span_x = pl.ds(pl.multiple_of(base + 112, 16), 96)
    landed("s4a")
    cs5a = {d: send("s5a", d - 1, ga, gath.at[span_a, lanes(y)], to_y(d)) for d in FAR_Y}
    gath[span_a, lanes(y)] = ga[...]
    landed("s4b")
    cs5b = {
        d: send("s5b", d - 1, gb.at[0:48, :], gath.at[span_b, lanes(z)], to_z(d)) for d in FAR_Y
    }
    gath[span_b, lanes(z)] = gb[0:48, :]
    landed("ry")
    rzs[...] = nn(perm[...], ryb[...].reshape(SLOTS, 128)).astype(BF16)
    for d in FAR_ZC:
        to = lax.rem(zc + d, NZC)
        send("rz", d - 1, rzs.at[y_rows(to), :], rzb.at[y_rows(zc), :], to_zc(d))
    rzb[y_rows(zc), :] = rzs[y_rows(zc), :]

    landed("s4x")
    for n in range(2):
        tiles = [gx8[n * 4 + g].astype(F32)[0:24] for g in range(4)]
        gx[:, n * 128 : (n + 1) * 128] = jnp.concatenate(tiles, axis=0).astype(BF16)
    cs5x = {d: send("s5x", d - 1, gx, gath.at[span_x, lanes(x, 256)], to_x(d)) for d in FAR_X}
    gath[span_x, lanes(x, 256)] = gx[...]

    pieces = [0]

    def forward(copies, d, span, coord, size):
        if d:
            copies[d].wait_recv()
        where = gath.at[span, lanes(lax.rem(coord - d + size, size), RELP // size)]
        send("s6", pieces[0], where, where, to_core)
        pieces[0] += 1

    for n, d in enumerate((0, 1, 7, 2, 6, 3, 5, 4)):
        forward(cs5a, d, span_a, y, NY)
        forward(cs5b, d, span_b, z, NY)
        if n % 2 == 0:
            forward(cs5x, (0, 1, 3, 2)[n // 2], span_x, x, NX)

    landed("rz")
    landed("lx")
    added = nn(ohsp[...], rzb[...]).T
    mine = (lg[x] + lgr[0]) + (lgr[1] + lgr[2])
    out_ent[...] = mine[0:QUARTER, :] + added[0:QUARTER, :]

    landed("s6")
    for n, stage in enumerate(STAGES):
        pltpu.make_async_copy(whole[stage], whole[stage], ssem.at[n]).wait()


PIECES = ((0, 0, 56), (64, 56, 48), (112, 104, 96), (208, 200, 56), (272, 256, 48), (320, 304, 96))


def finish(scale, ent, gath, out_ent, out_rel, wide, sems):
    copies = [pltpu.make_async_copy(ent, out_ent, sems.at[len(PIECES)])]
    copies[0].start()
    for n, (source, target, height) in enumerate(PIECES):
        rows = slice(target, target + height)
        wide[rows, :] = gath[source : source + height, 0:NREL].astype(F32) * F32(scale)
        copies.append(pltpu.make_async_copy(wide.at[rows, :], out_rel.at[rows, :], sems.at[n]))
        copies[-1].start()
    for copy in copies:
        copy.wait()


def shards(entities, relation, serve_ids, edge_src, edge_rel, edge_dst, neg_ids, edge_count):
    vmem = pl.BlockSpec(memory_space=pltpu.VMEM)
    v = pltpu.VMEM
    scratch = [
        v((D, SLOTS), BF16), v((2, 128), I32), v((1, EDGES), I32), v((1, EDGES), I32),
        v((1, EDGES), I32), v((2, 384), I32),
        v((D, NREL), F32), v((2, 128, 512), BF16), v((256, 256), BF16), v((2, 128, 256), BF16),
        v((256, 256), BF16), v((256, 256), BF16), v((256, 256), BF16), v((2, 128, 256), BF16),
        v((2, 128, 512), BF16), v((256, 256), BF16), v((256, 256), BF16), v((256, 256), BF16),
        v((SLOTS, EDGES), BF16), v((RELP, EDGES), BF16), v((D, EDGES), F32), v((D, EDGES), F32),
        v((D, EDGES), F32), v((D, EDGES), BF16), v((4, 128, EDGES), BF16),
        v((200, RELP), F32), v((200, RELP), F32), v((200, RELP), F32),
        v((7, 56, 128), F32), v((64, 128), F32), v((7, 48, 128), F32), v((64, 128), F32),
        v((3, 96, 256), F32), v((96, 256), F32),
        v((3, 16, 128), F32), v((3, 16, 128), F32), v((7, 24, 128), F32),
        v((8, 16, 128), F32), v((8, 16, 128), F32), v((8, 24, 128), F32),
        v((64, 128), BF16), v((64, 128), BF16), v((8, 32, 128), BF16), v((96, 256), BF16),
        v((4, 256, 128), F32), v((3, 256, 128), F32), v((2, 128, 128), BF16), v((2, 128, 128), BF16),
        v((256, 128), BF16), v((256, 128), BF16), v((4, 104, 256), F32), v((3, 104, 256), F32),
        pltpu.SemaphoreType.DMA((7,)), pltpu.SemaphoreType.DMA((len(STAGES),)), pltpu.SemaphoreType.DMA((ARRIVALS,)),
    ]
    operands = (
        entities.T, relation.T, serve_ids[0].T, edge_src[0], edge_rel[0], edge_dst[0],
        neg_ids[0, 0],
    )
    ent_t, gath = pl.pallas_call(
        kernel,
        out_shape=(
            jax.ShapeDtypeStruct((QUARTER, SLOTS), F32),
            jax.ShapeDtypeStruct((416, RELP), BF16),
        ),
        in_specs=[pl.BlockSpec(memory_space=pltpu.HBM)] * 7 + [pl.BlockSpec(memory_space=pltpu.SMEM)],
        out_specs=(vmem, vmem),
        scratch_shapes=scratch,
        compiler_params=pltpu.CompilerParams(
            collective_id=0, has_side_effects=True, vmem_limit_bytes=48 * 1024 * 1024
        ),
    )(
        *(pltpu.with_memory_space_constraint(a, pltpu.HBM) for a in operands), edge_count
    )
    slots = EDGES * lax.axis_size("dom") * lax.axis_size("rep")
    hbm = pl.BlockSpec(memory_space=pl.ANY)
    ent_t, rel_t = pl.pallas_call(
        functools.partial(finish, 1.0 / slots),
        out_shape=(
            jax.ShapeDtypeStruct((QUARTER, SLOTS), F32),
            jax.ShapeDtypeStruct((D, NREL), F32),
        ),
        in_specs=[vmem, vmem],
        out_specs=(hbm, hbm),
        scratch_shapes=[v((D, NREL), F32), pltpu.SemaphoreType.DMA((len(PIECES) + 1,))],
        compiler_params=pltpu.CompilerParams(vmem_limit_bytes=8 * 1024 * 1024),
    )(ent_t, gath)
    return ent_t.T, rel_t.T


def solution(mesh):
    placed = (
        P("dom", None),
        P(),
        P("dom", None, None),
        P("dom", "rep", None),
        P("dom", "rep", None),
        P("dom", "rep", None),
        P("dom", "rep", None, None),
        P("dom", "rep"),
    )
    return jax.shard_map(
        shards, mesh=mesh, in_specs=placed, out_specs=(P("dom", "rep"), P()), check_vma=False
    )
```

```python
import functools

import jax
import jax.numpy as jnp
from jax import lax
from jax.experimental import pallas as pl
from jax.experimental.pallas import tpu as pltpu
from jax.sharding import PartitionSpec as P

F32 = jnp.float32
BF16 = jnp.bfloat16
I32 = jnp.int32
NX, NY, NZC = 4, 8, 16
FAR_X, FAR_Y = (2, 1, 3), (4, 3, 5, 2, 6, 1, 7)
FAR_XY = sorted(
    ((dx, dy) for dx in range(4) for dy in range(8) if dx + dy),
    key=lambda move: (-min(move[0], 4 - move[0]) - min(move[1], 8 - move[1]), move),
)
FAR_ZC = (8, 7, 9, 6, 10, 5, 11, 4, 12, 3, 13, 2, 14, 1, 15)
D, NREL, RELP = 400, 1000, 1024
SLOTS, EDGES, BLOCK, GROUPS = 256, 512, 256, 2
QUARTER = 100
PART_A, PART_B = 64, 128
STAGES = (
    "a1", "a2", "b1", "b2", "core0", "core1", "core2", "s1a", "s1b", "s1x", "s2a", "s2b", "s2x",
    "s3a", "s3b", "s3x", "s4x", "s5a", "s5b", "s5x", "s6", "tx", "lx", "ry", "rz",
)
SINGLY = {"s5a": 0, "s5b": 8, "s5x": 16}
ARRIVALS = len(STAGES) + 19


def nn(a, b):
    return jnp.dot(a, b, preferred_element_type=F32)


def nt(a, b):
    return lax.dot_general(a, b, (((1,), (1,)), ((), ())), preferred_element_type=F32)


def split2(v):
    hi = v.astype(BF16)
    return hi, (v - hi.astype(F32)).astype(BF16)


def onehot(shape, axis, ids):
    return jnp.where(lax.broadcasted_iota(I32, shape, axis) == ids, F32(1), F32(0))


def kernel(
    ent_hbm, rel_hbm, serve_hbm, src_hbm, rel_ids_hbm, dst_hbm, neg_hbm, count,
    out_ent, gath,
    ent, serve, src, rel, dst, neg, relv, outs, outp, ra1, ra1p, ra2, rb1, rb1p, tab, perm, permt, ohsp,
    ohsrc, ohrel, fbuf, lhsv, relr, query, query4,
    rg, crecv, rgs, a1, a1s, b1, b1s, x1, x1s, a2, b2, x2, a3, b3, x3, ga, gb, gx8, gx,
    tg, tgb, tgr, tgs, ryb, rzs, rzb, lg, lgr,
    insem, ssem, rsem,
):
    me, x = lax.axis_index("dom"), lax.axis_index("rep")
    y, zc = me // NZC, lax.rem(me, NZC)
    z, c = zc // 2, lax.rem(zc, 2)

    def to_y(d):
        return {"dom": lax.rem(y + d, NY) * NZC + zc, "rep": x}

    def to_zc(d):
        return {"dom": y * NZC + lax.rem(zc + d, NZC), "rep": x}

    def to_z(d):
        return {"dom": y * NZC + lax.rem(z + d, NY) * 2 + c, "rep": x}

    def to_x(d):
        return {"dom": me, "rep": lax.rem(x + d, NX)}

    def to_yx(dx, d):
        return {"dom": lax.rem(y + d, NY) * NZC + zc, "rep": lax.rem(x + dx, NX)}

    def to_zx(dx, d):
        return {"dom": y * NZC + lax.rem(z + d, NY) * 2 + c, "rep": lax.rem(x + dx, NX)}

    to_core = {"dom": y * NZC + z * 2 + 1 - c, "rep": x}
    whole = {
        "a1": ra1.at[:, 0:112, :], "a2": ra2.at[0:240, :],
        "b1": rb1.at[0:240, :], "b2": tab.at[:, 0:112, 256:512],
        "core0": crecv.at[0:PART_A, :], "core1": crecv.at[PART_A:PART_B, :],
        "core2": crecv.at[PART_B:200, :],
        "s1a": a1, "s1b": b1, "s1x": x1, "s2a": a2, "s2b": b2, "s2x": x2,
        "s3a": a3.at[0:7], "s3b": b3.at[0:7], "s3x": x3.at[0:7],
        "s4x": gx8.at[0:7],
        "s5a": ohrel.at[0:496, 0:128], "s5b": ohrel.at[0:496, 0:128], "s5x": gath.at[0:80, 0:768],
        "s6": gath.at[0:208, :], "tx": tgr, "lx": lgr,
        "ry": ryb.at[:, 0:112, :], "rz": rzb.at[0:240, :],
    }

    def send(stage, i, source, target, device):
        n = STAGES.index(stage)
        arrival = len(STAGES) + SINGLY[stage] + i if stage in SINGLY else n
        copy = pltpu.make_async_remote_copy(
            src_ref=source, dst_ref=target, send_sem=ssem.at[n], recv_sem=rsem.at[arrival],
            device_id=device, device_id_type=pl.DeviceIdType.MESH,
        )
        copy.start()
        return copy

    def landed(stage):
        pltpu.make_async_copy(whole[stage], whole[stage], rsem.at[STAGES.index(stage)]).wait()

    barrier = pltpu.get_barrier_semaphore()
    partners = [to_y(d) for d in FAR_Y] + [to_zc(d) for d in FAR_ZC]
    partners += [to_x(d) for d in FAR_X]
    for device in partners:
        pl.semaphore_signal(barrier, inc=1, device_id=device, device_id_type=pl.DeviceIdType.MESH)

    fetches = []
    for n, (source, target) in enumerate((
        (ent_hbm, ent), (serve_hbm, serve), (src_hbm, src), (rel_ids_hbm, rel),
        (rel_hbm, relv), (dst_hbm, dst), (neg_hbm, neg),
    )):
        fetches.append(pltpu.make_async_copy(source, target, insem.at[n]))
        fetches[n].start()

    row = lax.broadcasted_iota(I32, (SLOTS, SLOTS), 0)
    col = lax.broadcasted_iota(I32, (SLOTS, SLOTS), 1)
    moved = ((col & 15) << 4) + ((col >> 7) << 3) + ((col >> 4) & 7)
    perm[...] = jnp.where(row == moved, F32(1), F32(0)).astype(BF16)
    fetches[1].wait()
    served = jnp.concatenate([serve[0:1, :], serve[1:2, :]], axis=1)
    ohst = jnp.where(row == served, F32(1), F32(0))
    ohs = ohst.T.astype(BF16)
    fetches[0].wait()
    outs[:, :, 384:512] = jnp.zeros((2, 128, 128), BF16)
    outs[:, :, 0:D] = nt(ohs, ent[...]).astype(BF16).reshape(2, 128, D)
    outp[:, 128:256] = jnp.zeros((SLOTS, 128), BF16)
    outp[:, 0 : D - 256] = nn(perm[...], outs[:, :, 256:D].reshape(SLOTS, D - 256)).astype(BF16)

    pl.semaphore_wait(barrier, len(partners))

    def y_rows(index):
        return pl.ds(pl.multiple_of(index * 16, 16), 16)

    for d in FAR_Y:
        to = lax.rem(y + d, NY)
        send("a1", d - 1, outs.at[:, y_rows(to), 0:256], ra1.at[:, y_rows(y), :], to_y(d))
    for d in FAR_ZC:
        to = lax.rem(zc + d, NZC)
        send("b1", d - 1, outp.at[y_rows(to), :], rb1.at[y_rows(zc), :], to_zc(d))
    ra1[:, y_rows(y), :] = outs[:, y_rows(y), 0:256]
    rb1[y_rows(zc), :] = outp[y_rows(zc), :]

    moved = ((row & 15) << 4) + ((row >> 7) << 3) + ((row >> 4) & 7)
    permt[...] = jnp.where(col == moved, F32(1), F32(0)).astype(BF16)
    ohsp[...] = nt(ohst.astype(BF16), perm[...]).astype(BF16)
    fetches[2].wait()
    ohsrc[...] = onehot((SLOTS, EDGES), 0, src[...]).astype(BF16)
    fbuf[...] = nn(ent[...], ohsrc[...])
    lhsv[...] = fbuf[...]
    fetches[3].wait()
    ohrel[...] = onehot((RELP, EDGES), 0, rel[...]).astype(BF16)
    fetches[4].wait()
    for q in range(4):
        part = relv[q * 104 : min(D, q * 104 + 104), :]
        hi = part.astype(BF16)
        rest = part - hi.astype(F32)
        mid = rest.astype(BF16)
        low = (rest - mid.astype(F32)).astype(BF16)
        picks = ohrel[0:NREL, :]
        relr[q * 104 : min(D, q * 104 + 104), :] = (nn(hi, picks) + nn(mid, picks)) + nn(low, picks)
    fbuf[...] = lhsv[...] * relr[...]
    query[...] = fbuf[...].astype(BF16)
    query4[...] = jnp.zeros(query4.shape, BF16)
    for q in range(4):
        query4[q, 0:QUARTER, :] = fbuf[q * QUARTER : (q + 1) * QUARTER, :].astype(BF16)

    for n in (5, 6):
        fetches[n].wait()
    live = lax.broadcasted_iota(I32, (1, EDGES), 1) < count[0, 0]
    livef = jnp.where(live, F32(1), F32(0))
    dsts = ((dst[...] & 1) << 7) + (dst[...] >> 1)
    negs = ((neg[...] & 1) << 7) + (neg[...] >> 1)
    ohdst = onehot((SLOTS, EDGES), 0, dsts) * livef
    times = []
    for b in range(GROUPS):
        ohneg = onehot((SLOTS, negs.shape[1]), 0, negs[b : b + 1, :])
        own = ohdst[:, b * BLOCK : (b + 1) * BLOCK]
        times.append(
            jnp.sum(ohneg, axis=1, keepdims=True) + jnp.sum(own, axis=1, keepdims=True)
        )

    landed("a1")
    ra1p[...] = nn(perm[...], ra1[...].reshape(SLOTS, 256)).astype(BF16)
    for d in FAR_ZC:
        to = lax.rem(zc + d, NZC)
        send("a2", d - 1, ra1p.at[y_rows(to), :], ra2.at[y_rows(zc), :], to_zc(d))
    ra2[y_rows(zc), :] = ra1p[y_rows(zc), :]
    landed("b1")
    rb1p[...] = nn(permt[...], rb1[...]).astype(BF16).reshape(2, 128, 256)
    for d in FAR_Y:
        to = lax.rem(y + d, NY)
        send("b2", d - 1, rb1p.at[:, y_rows(to), :], tab.at[:, y_rows(y), 256:512], to_y(d))
    tab[:, y_rows(y), 256:512] = rb1p[:, y_rows(y), :]
    landed("a2")
    tab[:, :, 0:256] = nn(permt[...], ra2[...]).astype(BF16).reshape(2, 128, 256)
    landed("b2")

    table = tab[...].reshape(SLOTS, 512)
    scores = nn(table[:, 0:D], query[...])
    his, los = [], []
    for b in range(GROUPS):
        span = slice(b * BLOCK, (b + 1) * BLOCK)
        s = jnp.where(times[b] > 0, scores[:, span], F32(-1e30))
        expo = jnp.exp(s - jnp.max(s, axis=0, keepdims=True))
        probs = expo / jnp.sum(expo * times[b], axis=0, keepdims=True)
        other = probs.astype(BF16).astype(F32)
        mine = (probs - F32(1)).astype(BF16).astype(F32)
        g = other * times[b] * livef[:, span] + ohdst[:, span] * (mine - other)
        hi, lo = split2(g)
        his.append(hi)
        los.append(lo)
    ghi = jnp.concatenate(his, axis=1)
    glo = jnp.concatenate(los, axis=1)
    tablet = table.astype(F32).T.astype(BF16)[0:D, :]
    dquery = nn(tablet, ghi) + nn(tablet, glo)
    fbuf[...] = dquery * lhsv[...]

    def rel_half(half):
        hi, lo = split2(fbuf[pl.ds(pl.multiple_of(half * 200, 8), 200), :])
        picks = ohrel[...]
        return nt(hi, picks) + nt(lo, picks)

    rows_a, rows_b, rows_x = slice(0, PART_A), slice(PART_A, PART_B), slice(PART_B, 200)
    rg[...] = rel_half(1 - c)
    for n, rows in enumerate((rows_a, rows_b, rows_x)):
        send("core%d" % n, 0, rg.at[rows, :], crecv.at[rows, :], to_core)
    rgs[...] = rel_half(c)

    grads = nt(ghi, query4[...].reshape(512, EDGES)) + nt(glo, query4[...].reshape(512, EDGES))
    for q in range(4):
        tg[q] = grads[:, q * 128 : (q + 1) * 128]
        tgb[q] = grads[:, q * 128 : (q + 1) * 128].astype(BF16)

    def lanes(index, width=128):
        return pl.ds(pl.multiple_of(index * width, 128), width)

    def reduce_first(part, stage, rows, buf, coord, size, to):
        landed("core%d" % part)
        rgs[rows, :] = rgs[rows, :] + crecv[rows, :]
        width = RELP // size
        for d in FAR_X if size == NX else FAR_Y:
            source = rgs.at[rows, lanes(lax.rem(coord + d, size), width)]
            send(stage, d - 1, source, buf.at[d - 1], to(d))

    reduce_first(0, "s1a", rows_a, a1, y, NY, to_y)
    reduce_first(1, "s1b", rows_b, b1, z, NY, to_z)
    reduce_first(2, "s1x", rows_x, x1, x, NX, to_x)
    for d in FAR_X:
        send("tx", d - 1, tgb.at[lax.rem(x + d, NX)], tgr.at[d - 1], to_x(d))
    hi, lo = split2(dquery * relr[...])
    relr[:, 0:SLOTS] = nt(hi, ohsrc[...]) + nt(lo, ohsrc[...])
    for q in range(4):
        lg[q, 0:QUARTER, :] = relr[q * QUARTER : (q + 1) * QUARTER, 0:SLOTS]
        lg[q, QUARTER:104, :] = jnp.zeros((104 - QUARTER, SLOTS), F32)

    def tile_of(index):
        group = pl.multiple_of(lax.rem(index, 4) * 24, 8)
        return pl.ds(group, 24), lanes(index // 4)

    landed("s1x")
    x1s[0:72, :] = (rgs[rows_x, lanes(x, 256)] + x1[0]) + (x1[1] + x1[2])
    x1s[72:96, :] = jnp.zeros((24, 256), F32)
    for d in FAR_Y:
        send("s2x", d - 1, x1s.at[tile_of(lax.rem(y + d, NY))], x2.at[d - 1], to_y(d))

    def reduce_second(first, stage, rows, buf, coord, total, buf2):
        landed(first)
        summed = rgs[rows, lanes(coord)]
        for d in range(NY - 1):
            summed = summed + buf[d]
        total[...] = summed
        for d in FAR_X:
            send(stage, d - 1, total.at[y_rows(lax.rem(x + d, NX)), :], buf2.at[d - 1], to_x(d))

    reduce_second("s1a", "s2a", rows_a, a1, y, a1s, a2)
    reduce_second("s1b", "s2b", rows_b, b1, z, b1s, b2)

    landed("tx")
    others = (tgr[0].astype(F32) + tgr[1].astype(F32)) + tgr[2].astype(F32)
    tgs[...] = (tg[x] + others).astype(BF16).reshape(2, 128, 128)
    for d in FAR_Y:
        to = lax.rem(y + d, NY)
        send("ry", d - 1, tgs.at[:, y_rows(to), :], ryb.at[:, y_rows(y), :], to_y(d))
    ryb[:, y_rows(y), :] = tgs[:, y_rows(y), :]

    def reduce_third(second, stage, total, buf2, buf3, coord, to):
        landed(second)
        buf3[coord] = (total[y_rows(x), :] + buf2[0]) + (buf2[1] + buf2[2])
        for d in FAR_Y:
            send(stage, d - 1, buf3.at[coord], buf3.at[coord], to(d))

    reduce_third("s2a", "s3a", a1s, a2, a3, z, to_z)
    reduce_third("s2b", "s3b", b1s, b2, b3, y, to_y)

    landed("s2x")
    sumx = x1s[tile_of(y)]
    for d in range(NY - 1):
        sumx = sumx + x2[d]
    x3[z] = sumx
    for d in FAR_Y:
        send("s3x", d - 1, x3.at[z], x3.at[z], to_z(d))

    for d in FAR_X:
        send("lx", d - 1, lg.at[lax.rem(x + d, NX)], lgr.at[d - 1], to_x(d))

    def sum8(buf):
        return ((buf[0] + buf[1]) + (buf[2] + buf[3])) + ((buf[4] + buf[5]) + (buf[6] + buf[7]))

    base = pl.multiple_of(c * 208, 16)
    span_a, span_b = pl.ds(base, 64), pl.ds(pl.multiple_of(base + 64, 16), 64)
    span_x = pl.ds(pl.multiple_of(base + 128, 16), 80)

    def gather(third, stage, buf3, own, first, coord, to):
        landed(third)
        own[...] = sum8(buf3).astype(BF16)
        rows = pl.ds(pl.multiple_of(base + first + x * 16, 16), 16)
        for dx, d in FAR_XY:
            send(stage, d, own, gath.at[rows, lanes(coord)], to(dx, d))
        gath[rows, lanes(coord)] = own[...]

    landed("s3x")
    gx8[y, 0:24, :] = sum8(x3).astype(BF16)
    gx8[y, 24:32, :] = jnp.zeros((8, 128), BF16)
    for d in FAR_Y:
        send("s4x", d - 1, gx8.at[y], gx8.at[y], to_y(d))
    gather("s3a", "s5a", a3, ga, 0, y, to_yx)
    gather("s3b", "s5b", b3, gb, 64, z, to_zx)

    landed("ry")
    rzs[...] = nn(perm[...], ryb[...].reshape(SLOTS, 128)).astype(BF16)
    for d in FAR_ZC:
        to = lax.rem(zc + d, NZC)
        send("rz", d - 1, rzs.at[y_rows(to), :], rzb.at[y_rows(zc), :], to_zc(d))
    rzb[y_rows(zc), :] = rzs[y_rows(zc), :]

    landed("s4x")
    for n in range(2):
        tiles = [gx8[n * 4 + g].astype(F32)[0:24] for g in range(4)]
        gx[:, n * 128 : (n + 1) * 128] = jnp.concatenate(tiles, axis=0)[0:80].astype(BF16)
    cs5x = {d: send("s5x", d - 1, gx, gath.at[span_x, lanes(x, 256)], to_x(d)) for d in FAR_X}
    gath[span_x, lanes(x, 256)] = gx[...]

    pieces = [0]

    def arrived(stage, d):
        block = gath.at[0:64, 0:128] if d else gath.at[0:48, 0:128]
        pltpu.make_async_copy(block, block, rsem.at[len(STAGES) + SINGLY[stage] + d]).wait()

    def forward(d, span, coord, size):
        where = gath.at[span, lanes(lax.rem(coord - d + size, size), RELP // size)]
        send("s6", pieces[0], where, where, to_core)
        pieces[0] += 1

    for n, d in enumerate((0, 1, 7, 2, 6, 3, 5, 4)):
        arrived("s5a", d)
        forward(d, span_a, y, NY)
        arrived("s5b", d)
        forward(d, span_b, z, NY)
        if n % 2 == 0:
            dx = (0, 1, 3, 2)[n // 2]
            if dx:
                cs5x[dx].wait_recv()
            forward(dx, span_x, x, NX)

    landed("rz")
    landed("lx")
    added = nn(ohsp[...], rzb[...]).T
    mine = (lg[x] + lgr[0]) + (lgr[1] + lgr[2])
    out_ent[...] = mine[0:QUARTER, :] + added[0:QUARTER, :]

    landed("s6")
    for n, stage in enumerate(STAGES):
        pltpu.make_async_copy(whole[stage], whole[stage], ssem.at[n]).wait()


PIECES = ((0, 0, 64), (64, 64, 64), (128, 128, 72), (208, 200, 64), (272, 264, 64), (336, 328, 72))


def finish(scale, ent, gath, out_ent, out_rel, wide, sems):
    copies = [pltpu.make_async_copy(ent, out_ent, sems.at[len(PIECES)])]
    copies[0].start()
    for n, (source, target, height) in enumerate(PIECES):
        rows = slice(target, target + height)
        wide[rows, :] = gath[source : source + height, 0:NREL].astype(F32) * F32(scale)
        copies.append(pltpu.make_async_copy(wide.at[rows, :], out_rel.at[rows, :], sems.at[n]))
        copies[-1].start()
    for copy in copies:
        copy.wait()


def shards(entities, relation, serve_ids, edge_src, edge_rel, edge_dst, neg_ids, edge_count):
    vmem = pl.BlockSpec(memory_space=pltpu.VMEM)
    v = pltpu.VMEM
    scratch = [
        v((D, SLOTS), BF16), v((2, 128), I32), v((1, EDGES), I32), v((1, EDGES), I32),
        v((1, EDGES), I32), v((2, 384), I32),
        v((D, NREL), F32), v((2, 128, 512), BF16), v((256, 256), BF16), v((2, 128, 256), BF16),
        v((256, 256), BF16), v((256, 256), BF16), v((256, 256), BF16), v((2, 128, 256), BF16),
        v((2, 128, 512), BF16), v((256, 256), BF16), v((256, 256), BF16), v((256, 256), BF16),
        v((SLOTS, EDGES), BF16), v((RELP, EDGES), BF16), v((D, EDGES), F32), v((D, EDGES), F32),
        v((D, EDGES), F32), v((D, EDGES), BF16), v((4, 128, EDGES), BF16),
        v((200, RELP), F32), v((200, RELP), F32), v((200, RELP), F32),
        v((7, 64, 128), F32), v((64, 128), F32), v((7, 64, 128), F32), v((64, 128), F32),
        v((3, 72, 256), F32), v((96, 256), F32),
        v((3, 16, 128), F32), v((3, 16, 128), F32), v((7, 24, 128), F32),
        v((8, 16, 128), F32), v((8, 16, 128), F32), v((8, 24, 128), F32),
        v((16, 128), BF16), v((16, 128), BF16), v((8, 32, 128), BF16), v((80, 256), BF16),
        v((4, 256, 128), F32), v((4, 256, 128), BF16), v((3, 256, 128), BF16), v((2, 128, 128), BF16), v((2, 128, 128), BF16),
        v((256, 128), BF16), v((256, 128), BF16), v((4, 104, 256), F32), v((3, 104, 256), F32),
        pltpu.SemaphoreType.DMA((7,)), pltpu.SemaphoreType.DMA((len(STAGES),)), pltpu.SemaphoreType.DMA((ARRIVALS,)),
    ]
    operands = (
        entities.T, relation.T, serve_ids[0].T, edge_src[0], edge_rel[0], edge_dst[0],
        neg_ids[0, 0],
    )
    ent_t, gath = pl.pallas_call(
        kernel,
        out_shape=(
            jax.ShapeDtypeStruct((QUARTER, SLOTS), F32),
            jax.ShapeDtypeStruct((416, RELP), BF16),
        ),
        in_specs=[pl.BlockSpec(memory_space=pltpu.HBM)] * 7 + [pl.BlockSpec(memory_space=pltpu.SMEM)],
        out_specs=(vmem, vmem),
        scratch_shapes=scratch,
        compiler_params=pltpu.CompilerParams(
            collective_id=0, has_side_effects=True, vmem_limit_bytes=48 * 1024 * 1024
        ),
    )(
        *(pltpu.with_memory_space_constraint(a, pltpu.HBM) for a in operands), edge_count
    )
    slots = EDGES * lax.axis_size("dom") * lax.axis_size("rep")
    hbm = pl.BlockSpec(memory_space=pl.ANY)
    ent_t, rel_t = pl.pallas_call(
        functools.partial(finish, 1.0 / slots),
        out_shape=(
            jax.ShapeDtypeStruct((QUARTER, SLOTS), F32),
            jax.ShapeDtypeStruct((D, NREL), F32),
        ),
        in_specs=[vmem, vmem],
        out_specs=(hbm, hbm),
        scratch_shapes=[v((D, NREL), F32), pltpu.SemaphoreType.DMA((len(PIECES) + 1,))],
        compiler_params=pltpu.CompilerParams(vmem_limit_bytes=8 * 1024 * 1024),
    )(ent_t, gath)
    return ent_t.T, rel_t.T


def solution(mesh):
    placed = (
        P("dom", None),
        P(),
        P("dom", None, None),
        P("dom", "rep", None),
        P("dom", "rep", None),
        P("dom", "rep", None),
        P("dom", "rep", None, None),
        P("dom", "rep"),
    )
    return jax.shard_map(
        shards, mesh=mesh, in_specs=placed, out_specs=(P("dom", "rep"), P()), check_vma=False
    )
```

```python
import functools

import jax
import jax.numpy as jnp
from jax import lax
from jax.experimental import pallas as pl
from jax.experimental.pallas import tpu as pltpu
from jax.sharding import PartitionSpec as P

F32 = jnp.float32
BF16 = jnp.bfloat16
I32 = jnp.int32
NX, NY, NZC = 4, 8, 16
FAR_X, FAR_Y = (2, 1, 3), (4, 3, 5, 2, 6, 1, 7)
FAR_XY = sorted(
    ((dx, dy) for dx in range(4) for dy in range(8) if dx + dy),
    key=lambda move: (-min(move[0], 4 - move[0]) - min(move[1], 8 - move[1]), move),
)
FAR_ZC = (8, 7, 9, 6, 10, 5, 11, 4, 12, 3, 13, 2, 14, 1, 15)
D, NREL, RELP = 400, 1000, 1024
SLOTS, EDGES, BLOCK, GROUPS = 256, 512, 256, 2
QUARTER = 100
PART_A, PART_B = 64, 128
STAGES = (
    "a1", "a2", "b1", "b2", "core0", "core1", "core2", "s1a", "s1b", "s1x", "s2a", "s2b", "s2x",
    "s3a", "s3b", "s3x", "s4x", "s5a", "s5b", "s5x", "s6", "tx", "lx", "ry", "rz",
)
SINGLY = {"s5a": 0, "s5b": 8, "s5x": 16}
ARRIVALS = len(STAGES) + 19


def nn(a, b):
    return jnp.dot(a, b, preferred_element_type=F32)


def nt(a, b):
    return lax.dot_general(a, b, (((1,), (1,)), ((), ())), preferred_element_type=F32)


def split2(v):
    hi = v.astype(BF16)
    return hi, (v - hi.astype(F32)).astype(BF16)


def onehot(shape, axis, ids):
    return jnp.where(lax.broadcasted_iota(I32, shape, axis) == ids, F32(1), F32(0))


def kernel(
    ent_hbm, rel_hbm, serve_hbm, src_hbm, rel_ids_hbm, dst_hbm, neg_hbm, count,
    out_ent, gath,
    ent, serve, src, rel, dst, neg, relv, outs, outp, ra1, ra1p, ra2, rb1, rb1p, tab, perm, permt, ohsp,
    ohsrc, ohrel, fbuf, wide, lhsv, relr, query, query4,
    rg, crecv, rgs, a1, a1s, b1, b1s, x1, x1s, a2, b2, x2, a3, b3, x3, ga, gb, gx8, gx,
    tg, tgb, tgr, tgs, ryb, rzs, rzb, lg, lgr,
    insem, ssem, rsem,
):
    me, x = lax.axis_index("dom"), lax.axis_index("rep")
    y, zc = me // NZC, lax.rem(me, NZC)
    z, c = zc // 2, lax.rem(zc, 2)

    def to_y(d):
        return {"dom": lax.rem(y + d, NY) * NZC + zc, "rep": x}

    def to_zc(d):
        return {"dom": y * NZC + lax.rem(zc + d, NZC), "rep": x}

    def to_z(d):
        return {"dom": y * NZC + lax.rem(z + d, NY) * 2 + c, "rep": x}

    def to_x(d):
        return {"dom": me, "rep": lax.rem(x + d, NX)}

    def to_yx(dx, d):
        return {"dom": lax.rem(y + d, NY) * NZC + zc, "rep": lax.rem(x + dx, NX)}

    def to_zx(dx, d):
        return {"dom": y * NZC + lax.rem(z + d, NY) * 2 + c, "rep": lax.rem(x + dx, NX)}

    to_core = {"dom": y * NZC + z * 2 + 1 - c, "rep": x}
    whole = {
        "a1": ra1.at[:, 0:112, :], "a2": ra2.at[0:240, :],
        "b1": rb1.at[0:240, :], "b2": tab.at[:, 0:112, 256:512],
        "core0": crecv.at[0:PART_A, :], "core1": crecv.at[PART_A:PART_B, :],
        "core2": crecv.at[PART_B:200, :],
        "s1a": a1, "s1b": b1, "s1x": x1, "s2a": a2, "s2b": b2, "s2x": x2,
        "s3a": a3.at[0:7], "s3b": b3.at[0:7], "s3x": x3.at[0:7],
        "s4x": gx8.at[0:7],
        "s5a": ohrel.at[0:496, 0:128], "s5b": ohrel.at[0:496, 0:128], "s5x": gath.at[0:80, 0:768],
        "s6": gath.at[0:208, :], "tx": tgr, "lx": lgr,
        "ry": ryb.at[:, 0:112, :], "rz": rzb.at[0:240, :],
    }

    def send(stage, i, source, target, device):
        n = STAGES.index(stage)
        arrival = len(STAGES) + SINGLY[stage] + i if stage in SINGLY else n
        copy = pltpu.make_async_remote_copy(
            src_ref=source, dst_ref=target, send_sem=ssem.at[n], recv_sem=rsem.at[arrival],
            device_id=device, device_id_type=pl.DeviceIdType.MESH,
        )
        copy.start()
        return copy

    def landed(stage):
        pltpu.make_async_copy(whole[stage], whole[stage], rsem.at[STAGES.index(stage)]).wait()

    barrier = pltpu.get_barrier_semaphore()
    partners = [to_y(d) for d in FAR_Y] + [to_zc(d) for d in FAR_ZC]
    partners += [to_x(d) for d in FAR_X]
    for device in partners:
        pl.semaphore_signal(barrier, inc=1, device_id=device, device_id_type=pl.DeviceIdType.MESH)

    fetches = []
    for n, (source, target) in enumerate((
        (ent_hbm, ent), (serve_hbm, serve), (src_hbm, src), (rel_ids_hbm, rel),
        (rel_hbm, relv), (dst_hbm, dst), (neg_hbm, neg),
    )):
        fetches.append(pltpu.make_async_copy(source, target, insem.at[n]))
        fetches[n].start()

    row = lax.broadcasted_iota(I32, (SLOTS, SLOTS), 0)
    col = lax.broadcasted_iota(I32, (SLOTS, SLOTS), 1)
    moved = ((col & 15) << 4) + ((col >> 7) << 3) + ((col >> 4) & 7)
    perm[...] = jnp.where(row == moved, F32(1), F32(0)).astype(BF16)
    fetches[1].wait()
    served = jnp.concatenate([serve[0:1, :], serve[1:2, :]], axis=1)
    ohst = jnp.where(row == served, F32(1), F32(0))
    ohs = ohst.T.astype(BF16)
    fetches[0].wait()
    outs[:, :, 384:512] = jnp.zeros((2, 128, 128), BF16)
    outs[:, :, 0:D] = nt(ohs, ent[...]).astype(BF16).reshape(2, 128, D)
    outp[:, 128:256] = jnp.zeros((SLOTS, 128), BF16)
    outp[:, 0 : D - 256] = nn(perm[...], outs[:, :, 256:D].reshape(SLOTS, D - 256)).astype(BF16)

    pl.semaphore_wait(barrier, len(partners))

    def y_rows(index):
        return pl.ds(pl.multiple_of(index * 16, 16), 16)

    for d in FAR_Y:
        to = lax.rem(y + d, NY)
        send("a1", d - 1, outs.at[:, y_rows(to), 0:256], ra1.at[:, y_rows(y), :], to_y(d))
    for d in FAR_ZC:
        to = lax.rem(zc + d, NZC)
        send("b1", d - 1, outp.at[y_rows(to), :], rb1.at[y_rows(zc), :], to_zc(d))
    ra1[:, y_rows(y), :] = outs[:, y_rows(y), 0:256]
    rb1[y_rows(zc), :] = outp[y_rows(zc), :]

    moved = ((row & 15) << 4) + ((row >> 7) << 3) + ((row >> 4) & 7)
    permt[...] = jnp.where(col == moved, F32(1), F32(0)).astype(BF16)
    ohsp[...] = nt(ohst.astype(BF16), perm[...]).astype(BF16)
    fetches[2].wait()
    ohsrc[...] = onehot((SLOTS, EDGES), 0, src[...]).astype(BF16)
    fbuf[...] = nn(ent[...], ohsrc[...])
    lhsv[...] = fbuf[...]
    fetches[3].wait()
    ohrel[...] = onehot((RELP, EDGES), 0, rel[...]).astype(BF16)
    fetches[4].wait()
    for q in range(4):
        part = relv[q * 104 : min(D, q * 104 + 104), :]
        hi = part.astype(BF16)
        rest = part - hi.astype(F32)
        mid = rest.astype(BF16)
        low = (rest - mid.astype(F32)).astype(BF16)
        picks = ohrel[0:NREL, :]
        relr[q * 104 : min(D, q * 104 + 104), :] = (nn(hi, picks) + nn(mid, picks)) + nn(low, picks)
    fbuf[...] = lhsv[...] * relr[...]
    query[...] = fbuf[...].astype(BF16)
    query4[...] = jnp.zeros(query4.shape, BF16)
    for q in range(4):
        query4[q, 0:QUARTER, :] = fbuf[q * QUARTER : (q + 1) * QUARTER, :].astype(BF16)

    for n in (5, 6):
        fetches[n].wait()
    live = lax.broadcasted_iota(I32, (1, EDGES), 1) < count[0, 0]
    livef = jnp.where(live, F32(1), F32(0))
    dsts = ((dst[...] & 1) << 7) + (dst[...] >> 1)
    negs = ((neg[...] & 1) << 7) + (neg[...] >> 1)
    ohdst = onehot((SLOTS, EDGES), 0, dsts) * livef
    times = []
    for b in range(GROUPS):
        ohneg = onehot((SLOTS, negs.shape[1]), 0, negs[b : b + 1, :])
        own = ohdst[:, b * BLOCK : (b + 1) * BLOCK]
        times.append(
            jnp.sum(ohneg, axis=1, keepdims=True) + jnp.sum(own, axis=1, keepdims=True)
        )

    landed("a1")
    ra1p[...] = nn(perm[...], ra1[...].reshape(SLOTS, 256)).astype(BF16)
    for d in FAR_ZC:
        to = lax.rem(zc + d, NZC)
        send("a2", d - 1, ra1p.at[y_rows(to), :], ra2.at[y_rows(zc), :], to_zc(d))
    ra2[y_rows(zc), :] = ra1p[y_rows(zc), :]
    landed("b1")
    rb1p[...] = nn(permt[...], rb1[...]).astype(BF16).reshape(2, 128, 256)
    for d in FAR_Y:
        to = lax.rem(y + d, NY)
        send("b2", d - 1, rb1p.at[:, y_rows(to), :], tab.at[:, y_rows(y), 256:512], to_y(d))
    tab[:, y_rows(y), 256:512] = rb1p[:, y_rows(y), :]
    landed("a2")
    tab[:, :, 0:256] = nn(permt[...], ra2[...]).astype(BF16).reshape(2, 128, 256)
    landed("b2")

    table = tab[...].reshape(SLOTS, 512)
    scores = nn(table[:, 0:D], query[...])
    his, los = [], []
    for b in range(GROUPS):
        span = slice(b * BLOCK, (b + 1) * BLOCK)
        s = jnp.where(times[b] > 0, scores[:, span], F32(-1e30))
        expo = jnp.exp(s - jnp.max(s, axis=0, keepdims=True))
        probs = expo / jnp.sum(expo * times[b], axis=0, keepdims=True)
        other = probs.astype(BF16).astype(F32)
        mine = (probs - F32(1)).astype(BF16).astype(F32)
        g = other * times[b] * livef[:, span] + ohdst[:, span] * (mine - other)
        hi, lo = split2(g)
        his.append(hi)
        los.append(lo)
    ghi = jnp.concatenate(his, axis=1)
    glo = jnp.concatenate(los, axis=1)
    tablet = table.astype(F32).T.astype(BF16)[0:D, :]
    dquery = nn(tablet, ghi) + nn(tablet, glo)
    wide[0:D, :] = dquery * lhsv[...]
    wide[D:408, :] = jnp.zeros((8, EDGES), F32)

    def rel_half(half):
        terms = split2(wide[pl.ds(pl.multiple_of(half * 200, 8), 208), :])
        both = nt(jnp.concatenate(terms, axis=0), ohrel[...])
        return both[0:200] + both[208:408]

    rows_a, rows_b, rows_x = slice(0, PART_A), slice(PART_A, PART_B), slice(PART_B, 200)
    rg[...] = rel_half(1 - c)
    for n, rows in enumerate((rows_a, rows_b, rows_x)):
        send("core%d" % n, 0, rg.at[rows, :], crecv.at[rows, :], to_core)
    rgs[...] = rel_half(c)

    both = nt(jnp.concatenate([ghi, glo], axis=0), query4[...].reshape(512, EDGES))
    grads = both[0:SLOTS] + both[SLOTS:]
    for q in range(4):
        tg[q] = grads[:, q * 128 : (q + 1) * 128]
        tgb[q] = grads[:, q * 128 : (q + 1) * 128].astype(BF16)

    def lanes(index, width=128):
        return pl.ds(pl.multiple_of(index * width, 128), width)

    def reduce_first(part, stage, rows, buf, coord, size, to):
        landed("core%d" % part)
        rgs[rows, :] = rgs[rows, :] + crecv[rows, :]
        width = RELP // size
        for d in FAR_X if size == NX else FAR_Y:
            source = rgs.at[rows, lanes(lax.rem(coord + d, size), width)]
            send(stage, d - 1, source, buf.at[d - 1], to(d))

    reduce_first(0, "s1a", rows_a, a1, y, NY, to_y)
    reduce_first(1, "s1b", rows_b, b1, z, NY, to_z)
    reduce_first(2, "s1x", rows_x, x1, x, NX, to_x)
    for d in FAR_X:
        send("tx", d - 1, tgb.at[lax.rem(x + d, NX)], tgr.at[d - 1], to_x(d))
    hi, lo = split2(dquery * relr[...])
    relr[:, 0:SLOTS] = nt(hi, ohsrc[...]) + nt(lo, ohsrc[...])
    for q in range(4):
        lg[q, 0:QUARTER, :] = relr[q * QUARTER : (q + 1) * QUARTER, 0:SLOTS]
        lg[q, QUARTER:104, :] = jnp.zeros((104 - QUARTER, SLOTS), F32)

    def tile_of(index):
        group = pl.multiple_of(lax.rem(index, 4) * 24, 8)
        return pl.ds(group, 24), lanes(index // 4)

    landed("s1x")
    x1s[0:72, :] = (rgs[rows_x, lanes(x, 256)] + x1[0]) + (x1[1] + x1[2])
    x1s[72:96, :] = jnp.zeros((24, 256), F32)
    for d in FAR_Y:
        send("s2x", d - 1, x1s.at[tile_of(lax.rem(y + d, NY))], x2.at[d - 1], to_y(d))

    def reduce_second(first, stage, rows, buf, coord, total, buf2):
        landed(first)
        summed = rgs[rows, lanes(coord)]
        for d in range(NY - 1):
            summed = summed + buf[d]
        total[...] = summed
        for d in FAR_X:
            send(stage, d - 1, total.at[y_rows(lax.rem(x + d, NX)), :], buf2.at[d - 1], to_x(d))

    reduce_second("s1a", "s2a", rows_a, a1, y, a1s, a2)
    reduce_second("s1b", "s2b", rows_b, b1, z, b1s, b2)

    landed("tx")
    others = (tgr[0].astype(F32) + tgr[1].astype(F32)) + tgr[2].astype(F32)
    tgs[...] = (tg[x] + others).astype(BF16).reshape(2, 128, 128)
    for d in FAR_Y:
        to = lax.rem(y + d, NY)
        send("ry", d - 1, tgs.at[:, y_rows(to), :], ryb.at[:, y_rows(y), :], to_y(d))
    ryb[:, y_rows(y), :] = tgs[:, y_rows(y), :]

    landed("s2x")
    sumx = x1s[tile_of(y)]
    for d in range(NY - 1):
        sumx = sumx + x2[d]
    x3[z] = sumx
    for d in FAR_Y:
        send("s3x", d - 1, x3.at[z], x3.at[z], to_z(d))

    def reduce_third(second, stage, total, buf2, buf3, coord, to):
        landed(second)
        buf3[coord] = (total[y_rows(x), :] + buf2[0]) + (buf2[1] + buf2[2])
        for d in FAR_Y:
            send(stage, d - 1, buf3.at[coord], buf3.at[coord], to(d))

    reduce_third("s2a", "s3a", a1s, a2, a3, z, to_z)
    reduce_third("s2b", "s3b", b1s, b2, b3, y, to_y)

    for d in FAR_X:
        send("lx", d - 1, lg.at[lax.rem(x + d, NX)], lgr.at[d - 1], to_x(d))

    def sum8(buf):
        return ((buf[0] + buf[1]) + (buf[2] + buf[3])) + ((buf[4] + buf[5]) + (buf[6] + buf[7]))

    base = pl.multiple_of(c * 208, 16)
    span_a, span_b = pl.ds(base, 64), pl.ds(pl.multiple_of(base + 64, 16), 64)
    span_x = pl.ds(pl.multiple_of(base + 128, 16), 80)

    def gather(third, stage, buf3, own, first, coord, to):
        landed(third)
        own[...] = sum8(buf3).astype(BF16)
        rows = pl.ds(pl.multiple_of(base + first + x * 16, 16), 16)
        for dx, d in FAR_XY:
            send(stage, d, own, gath.at[rows, lanes(coord)], to(dx, d))
        gath[rows, lanes(coord)] = own[...]

    landed("s3x")
    gx8[y, 0:24, :] = sum8(x3).astype(BF16)
    gx8[y, 24:32, :] = jnp.zeros((8, 128), BF16)
    for d in FAR_Y:
        send("s4x", d - 1, gx8.at[y], gx8.at[y], to_y(d))
    gather("s3a", "s5a", a3, ga, 0, y, to_yx)
    gather("s3b", "s5b", b3, gb, 64, z, to_zx)

    landed("ry")
    rzs[...] = nn(perm[...], ryb[...].reshape(SLOTS, 128)).astype(BF16)
    for d in FAR_ZC:
        to = lax.rem(zc + d, NZC)
        send("rz", d - 1, rzs.at[y_rows(to), :], rzb.at[y_rows(zc), :], to_zc(d))
    rzb[y_rows(zc), :] = rzs[y_rows(zc), :]

    landed("s4x")
    for n in range(2):
        tiles = [gx8[n * 4 + g].astype(F32)[0:24] for g in range(4)]
        gx[:, n * 128 : (n + 1) * 128] = jnp.concatenate(tiles, axis=0)[0:80].astype(BF16)
    cs5x = {d: send("s5x", d - 1, gx, gath.at[span_x, lanes(x, 256)], to_x(d)) for d in FAR_X}
    gath[span_x, lanes(x, 256)] = gx[...]

    pieces = [0]

    def arrived(stage, d):
        block = gath.at[0:64, 0:128] if d else gath.at[0:48, 0:128]
        pltpu.make_async_copy(block, block, rsem.at[len(STAGES) + SINGLY[stage] + d]).wait()

    def forward(d, span, coord, size):
        where = gath.at[span, lanes(lax.rem(coord - d + size, size), RELP // size)]
        send("s6", pieces[0], where, where, to_core)
        pieces[0] += 1

    forward(0, span_x, x, NX)
    for d in (0, 1, 7, 2, 6, 3, 5, 4):
        arrived("s5a", d)
        forward(d, span_a, y, NY)
        arrived("s5b", d)
        forward(d, span_b, z, NY)
    for dx in (1, 3, 2):
        cs5x[dx].wait_recv()
        forward(dx, span_x, x, NX)

    landed("rz")
    landed("lx")
    added = nn(ohsp[...], rzb[...]).T
    mine = (lg[x] + lgr[0]) + (lgr[1] + lgr[2])
    out_ent[...] = mine[0:QUARTER, :] + added[0:QUARTER, :]

    landed("s6")
    for n, stage in enumerate(STAGES):
        pltpu.make_async_copy(whole[stage], whole[stage], ssem.at[n]).wait()


PIECES = ((0, 0, 64), (64, 64, 64), (128, 128, 72), (208, 200, 64), (272, 264, 64), (336, 328, 72))


def finish(scale, ent, gath, out_ent, out_rel, wide, sems):
    copies = [pltpu.make_async_copy(ent, out_ent, sems.at[len(PIECES)])]
    copies[0].start()
    for n, (source, target, height) in enumerate(PIECES):
        rows = slice(target, target + height)
        wide[rows, :] = gath[source : source + height, 0:NREL].astype(F32) * F32(scale)
        copies.append(pltpu.make_async_copy(wide.at[rows, :], out_rel.at[rows, :], sems.at[n]))
        copies[-1].start()
    for copy in copies:
        copy.wait()


def shards(entities, relation, serve_ids, edge_src, edge_rel, edge_dst, neg_ids, edge_count):
    vmem = pl.BlockSpec(memory_space=pltpu.VMEM)
    v = pltpu.VMEM
    scratch = [
        v((D, SLOTS), BF16), v((2, 128), I32), v((1, EDGES), I32), v((1, EDGES), I32),
        v((1, EDGES), I32), v((2, 384), I32),
        v((D, NREL), F32), v((2, 128, 512), BF16), v((256, 256), BF16), v((2, 128, 256), BF16),
        v((256, 256), BF16), v((256, 256), BF16), v((256, 256), BF16), v((2, 128, 256), BF16),
        v((2, 128, 512), BF16), v((256, 256), BF16), v((256, 256), BF16), v((256, 256), BF16),
        v((SLOTS, EDGES), BF16), v((RELP, EDGES), BF16), v((D, EDGES), F32), v((408, EDGES), F32), v((D, EDGES), F32),
        v((D, EDGES), F32), v((D, EDGES), BF16), v((4, 128, EDGES), BF16),
        v((200, RELP), F32), v((200, RELP), F32), v((200, RELP), F32),
        v((7, 64, 128), F32), v((64, 128), F32), v((7, 64, 128), F32), v((64, 128), F32),
        v((3, 72, 256), F32), v((96, 256), F32),
        v((3, 16, 128), F32), v((3, 16, 128), F32), v((7, 24, 128), F32),
        v((8, 16, 128), F32), v((8, 16, 128), F32), v((8, 24, 128), F32),
        v((16, 128), BF16), v((16, 128), BF16), v((8, 32, 128), BF16), v((80, 256), BF16),
        v((4, 256, 128), F32), v((4, 256, 128), BF16), v((3, 256, 128), BF16), v((2, 128, 128), BF16), v((2, 128, 128), BF16),
        v((256, 128), BF16), v((256, 128), BF16), v((4, 104, 256), F32), v((3, 104, 256), F32),
        pltpu.SemaphoreType.DMA((7,)), pltpu.SemaphoreType.DMA((len(STAGES),)), pltpu.SemaphoreType.DMA((ARRIVALS,)),
    ]
    operands = (
        entities.T, relation.T, serve_ids[0].T, edge_src[0], edge_rel[0], edge_dst[0],
        neg_ids[0, 0],
    )
    ent_t, gath = pl.pallas_call(
        kernel,
        out_shape=(
            jax.ShapeDtypeStruct((QUARTER, SLOTS), F32),
            jax.ShapeDtypeStruct((416, RELP), BF16),
        ),
        in_specs=[pl.BlockSpec(memory_space=pltpu.HBM)] * 7 + [pl.BlockSpec(memory_space=pltpu.SMEM)],
        out_specs=(vmem, vmem),
        scratch_shapes=scratch,
        compiler_params=pltpu.CompilerParams(
            collective_id=0, has_side_effects=True, vmem_limit_bytes=48 * 1024 * 1024
        ),
    )(
        *(pltpu.with_memory_space_constraint(a, pltpu.HBM) for a in operands), edge_count
    )
    slots = EDGES * lax.axis_size("dom") * lax.axis_size("rep")
    hbm = pl.BlockSpec(memory_space=pl.ANY)
    ent_t, rel_t = pl.pallas_call(
        functools.partial(finish, 1.0 / slots),
        out_shape=(
            jax.ShapeDtypeStruct((QUARTER, SLOTS), F32),
            jax.ShapeDtypeStruct((D, NREL), F32),
        ),
        in_specs=[vmem, vmem],
        out_specs=(hbm, hbm),
        scratch_shapes=[v((D, NREL), F32), pltpu.SemaphoreType.DMA((len(PIECES) + 1,))],
        compiler_params=pltpu.CompilerParams(vmem_limit_bytes=8 * 1024 * 1024),
    )(ent_t, gath)
    return ent_t.T, rel_t.T


def solution(mesh):
    placed = (
        P("dom", None),
        P(),
        P("dom", None, None),
        P("dom", "rep", None),
        P("dom", "rep", None),
        P("dom", "rep", None),
        P("dom", "rep", None, None),
        P("dom", "rep"),
    )
    return jax.shard_map(
        shards, mesh=mesh, in_specs=placed, out_specs=(P("dom", "rep"), P()), check_vma=False
    )
```
